32 devices in a mesh: cell: 2 (over core), gene: 4 (over y, x), rank: 4 (over z).
Axes of the slice: x: 2, y: 2, z: 4, core: 2. Of those that a mesh axis runs over, the one named last changes fastest.
Arguments:
- blocks: bfloat16 [2, 16, 96, 256, 128], P('cell', ('gene', 'rank')), may hold values from -6 to 6
- block_pos: int32 [2, 16, 96], P('cell', ('gene', 'rank')), may hold values from 0 to 127, as said below
- block_count: int32 [2, 16], P('cell', ('gene', 'rank')), may hold values from 32 to 96, as said below
- test_right: bfloat16 [32768, 512], P(('gene', 'rank')), may hold values from -0.0625 to 0.0625
- test_left: bfloat16 [4096, 768], P('cell', 'rank'), may hold values from -0.1875 to 0.1875
- gene_sketch_old: float32 [768, 32768], P('cell', ('gene', 'rank')), may hold values from -4 to 4
Outputs:
- right_sketch: float32 [4096, 512], P(('cell', 'gene', 'rank'))
- gene_sketch: float32 [768, 32768], P('cell', ('gene', 'rank'))
- core: float32 [768, 512], P('cell')
The draws below stay inside these ranges and needn't reach their ends.
Inputs may be any that keep to these rules, and one draw needn't show every extreme that they name: `block_pos`: position p names row block p // 16 and gene block p % 16 of the device's tile; the 96 positions of one device are distinct. `block_count`: some device has all 96 slots live in every draw; slots from the count on are not part of A.
All inputs are finite; a program needn't handle non-finite values.
Results may differ from the reference program's by a relative error of at most 0.0003.
Values may be sent and summed in bfloat16 or wider, within the bound.
A program may use at most 128 MiB of HBM per device.

```python
import jax
import jax.numpy as jnp
from jax import lax

BROWS = 256
BCOLS = 128
R = 512
L = 768
GB_DEV = 16
RB_DEV = 8
NB = 96
CSHARDS = 2
GSHARDS = 16
CELLS = 4096
GENES = 32768
N_CELL = 2
N_GENE = 4
N_RANK = 4


def draw_block_pos(key, part):
    devices = CSHARDS * GSHARDS
    tile_size = RB_DEV * GB_DEV
    subkeys = jax.random.split(key, devices)
    orders = jax.vmap(lambda single: jax.random.permutation(single, tile_size))(subkeys)
    return orders[:, :NB].reshape(CSHARDS, GSHARDS, NB).astype(jnp.int32)


def draw_block_count(key, part):
    first_key, second_key = jax.random.split(jax.random.fold_in(key, 7))
    devices = CSHARDS * GSHARDS
    spread = jax.random.randint(first_key, (devices,), 0, 65)
    floor_count = NB // 3
    counts = floor_count + (NB - floor_count) * spread * spread // 4096
    chosen = jax.random.randint(second_key, (), 0, devices)
    counts = jnp.where(jnp.arange(devices) == chosen, NB, counts)
    return counts.reshape(CSHARDS, GSHARDS).astype(jnp.int32)


def block_scale(stream_key, extent, cuts, least, high):
    gain = 1.0
    for dim, shards_of in cuts:
        heights = jax.random.uniform(jax.random.fold_in(jax.random.fold_in(stream_key, 6), dim), (shards_of,), jnp.float32, least / len(cuts), high / len(cuts))
        gain = gain * jnp.repeat(jnp.exp(heights), extent[dim] // shards_of).reshape((-1,) + (1,) * (len(extent) - 1 - dim))
    return gain


def scatter_about(stream_key, extent, deviation, bound, pieces=(), kind=jnp.bfloat16):
    loudness = block_scale(stream_key, extent, pieces, -0.22, 0.18) if pieces else 1.0
    values = jax.random.normal(stream_key, extent, jnp.float32) * deviation * loudness
    return jnp.minimum(jnp.maximum(values, -bound), bound).astype(kind)


def setup_inputs(seed: int = 0) -> dict:
    key_list = jax.random.split(jax.random.key(seed), 7)
    return {
        "blocks": scatter_about(key_list[0], (N_CELL, N_GENE * N_RANK, NB, BROWS, BCOLS), 1.0, 6.0, ((0, 2), (1, 16))),
        "block_pos": draw_block_pos(jax.random.fold_in(key_list[6], 71), 0),
        "block_count": draw_block_count(jax.random.fold_in(key_list[6], 71), 0),
        "test_right": scatter_about(key_list[3], (GENES, R), (GENES // 4) ** -0.5, 0.0625, ((0, 16),)),
        "test_left": scatter_about(key_list[4], (CELLS, L), (CELLS // 4) ** -0.5, 0.1875, ((0, 2), (1, 4))),
        "gene_sketch_old": scatter_about(key_list[5], (L, GENES), 0.5, 4.0, ((0, 2), (1, 16)), jnp.float32),
    }


def reference(blocks, block_pos, block_count, test_right, test_left, gene_sketch_old):
    highest = lax.Precision.HIGHEST
    cell_rows = RB_DEV * BROWS
    gene_cols = GB_DEV * BCOLS
    right_table = test_right.reshape(GSHARDS * GB_DEV, BCOLS, R)
    left_table = test_left.reshape(CSHARDS * RB_DEV, BROWS, L)
    slot_ids = jnp.arange(NB, dtype=jnp.int32)
    row_ids = jnp.arange(RB_DEV, dtype=jnp.int32)
    gene_ids = jnp.arange(GB_DEV, dtype=jnp.int32)

    def visit(carry, flat_index):
        right_acc, gene_acc = carry
        cell_index = flat_index // GSHARDS
        gene_index = flat_index % GSHARDS
        tiles = blocks[cell_index, gene_index].astype(jnp.float32)
        positions = block_pos[cell_index, gene_index]
        alive_mask = (slot_ids < block_count[cell_index, gene_index]).astype(jnp.float32)
        row_block = positions // GB_DEV
        gene_block = positions % GB_DEV
        right_rows = right_table[gene_index * GB_DEV + gene_block].astype(jnp.float32)
        left_rows = left_table[cell_index * RB_DEV + row_block].astype(jnp.float32)
        right_terms = jnp.einsum("pik,pkr->pir", tiles, right_rows, precision=highest) * alive_mask[:, None, None]
        gene_terms = jnp.einsum("pil,pik->plk", left_rows, tiles, precision=highest) * alive_mask[:, None, None]
        row_hot = (row_block[None, :] == row_ids[:, None]).astype(jnp.float32)
        gene_hot = (gene_block[None, :] == gene_ids[:, None]).astype(jnp.float32)
        right_tile = jnp.einsum("rp,pik->rik", row_hot, right_terms, precision=highest).reshape(cell_rows, R)
        gene_tile = jnp.einsum("gp,plk->lgk", gene_hot, gene_terms, precision=highest).reshape(L, gene_cols)
        row_start = (cell_index * cell_rows).astype(jnp.int32)
        col_start = (gene_index * gene_cols).astype(jnp.int32)
        anchor = jnp.zeros((), jnp.int32)
        old_rows = lax.dynamic_slice(right_acc, (row_start, anchor), (cell_rows, R))
        right_acc = lax.dynamic_update_slice(right_acc, old_rows + right_tile, (row_start, anchor))
        old_cols = lax.dynamic_slice(gene_acc, (anchor, col_start), (L, gene_cols))
        gene_acc = lax.dynamic_update_slice(gene_acc, old_cols + gene_tile, (anchor, col_start))
        return (right_acc, gene_acc), None

    initial = (jnp.zeros((CSHARDS * cell_rows, R), jnp.float32), jnp.zeros((L, GSHARDS * gene_cols), jnp.float32))
    (right_sketch, gene_sum), unused = lax.scan(visit, initial, jnp.arange(CSHARDS * GSHARDS, dtype=jnp.int32))
    core = lax.dot_general(test_left.astype(jnp.float32), right_sketch, (((0,), (0,)), ((), ())), precision=highest)
    return right_sketch, gene_sketch_old + gene_sum, core
```

```python
import functools

import jax
import jax.numpy as jnp
from jax import lax
from jax.experimental import pallas as pl
from jax.experimental.pallas import tpu as pltpu
from jax.sharding import PartitionSpec as P

MESH = pl.DeviceIdType.MESH
GENE_CHUNK = 1024
TOP = 32767.0


def encode(x):
    peak = jnp.maximum(jnp.max(jnp.abs(x), axis=0, keepdims=True), 1e-30)
    codes = jnp.round(x * (TOP / peak)).astype(jnp.int32).astype(jnp.int16)
    return codes, peak * (1.0 / TOP)


def decode(codes, step):
    return codes.astype(jnp.int32).astype(jnp.float32) * step


class Group:
    def __init__(self, *copies):
        self.copies = copies

    def start(self):
        for copy in self.copies:
            copy.start()
        return self

    def wait_recv(self):
        for copy in self.copies:
            copy.wait_recv()

    def wait_send(self):
        for copy in self.copies:
            copy.wait_send()


def kernel(
    sizes, code, blocks, right_in, left_in, old_in, right_out, gene_out, core_out,
    tiles, dense, table, left, part, one_s, one_r, one_ss, one_sr, two_s, two_r, two_ss, two_sr,
    z_s, z_r, z_ss, z_sr, core_part, core_cell, cg_c, cg_d, cg_cs, cg_ds, cr_c, cr_d, cr_cs, cr_ds,
    core_code, core_step, gene_send, gene_recv,
    load_sem, agz_s, agz_r, agx_s, agx_r, agd_s, agd_r, rs1_s, rs1_r, rs2_s, rs2_r, rsz_s, rsz_r,
    cc_s, cc_r, cgs_s, cgs_r, crs_s, crs_r, ar_s, ar_r, ag_s, ag_r, gs_s, gs_r,
):
    n_cell, n_gene, n_rank = sizes
    f32, bf16 = jnp.float32, jnp.bfloat16
    c, g, r = lax.axis_index("cell"), lax.axis_index("gene"), lax.axis_index("rank")
    b1, b0 = g // 2, g % 2
    gx = 2 * b1 + (1 - b0)
    gy = 2 * (1 - b1) + b0
    gd = 2 * (1 - b1) + (1 - b0)
    gene_peers = [gx, gy, gd]
    rows, width = part.shape
    quarter = rows // n_gene
    shard = quarter // n_rank
    half = width // 2
    lw = left_in.shape[0]
    left_width = left.shape[0]
    brows, bcols = tiles.shape[1], tiles.shape[2]
    gene_blocks = dense.shape[1] // bcols
    share = left_width // n_cell
    core_rows = share // n_gene
    lanes = width // n_rank

    def rank_of(k):
        return lax.rem(r + k, n_rank)

    def cell_of(k):
        return lax.rem(c + k, n_cell)

    def cut(start, step):
        return pl.ds(pl.multiple_of(start * step, step), step)

    def remote(src, dst, ssem, rsem, **where):
        device = (where.get("cell", c), where.get("gene", g), where.get("rank", r))
        return pltpu.make_async_remote_copy(
            src_ref=src, dst_ref=dst, send_sem=ssem, recv_sem=rsem,
            device_id=device, device_id_type=MESH,
        )

    def ship(codes, steps, ssem, rsem, **where):
        return Group(
            remote(*codes, ssem.at[0], rsem.at[0], **where),
            remote(*steps, ssem.at[1], rsem.at[1], **where),
        ).start()

    barrier = pltpu.get_barrier_semaphore()
    for k in range(1, n_rank):
        pl.semaphore_signal(barrier, inc=1, device_id=(c, g, rank_of(k)), device_id_type=MESH)
    for peer in gene_peers:
        pl.semaphore_signal(barrier, inc=1, device_id=(c, peer, r), device_id_type=MESH)
    for k in range(1, n_cell):
        pl.semaphore_signal(barrier, inc=1, device_id=(cell_of(k), g, r), device_id_type=MESH)

    load_tiles = pltpu.make_async_copy(blocks, tiles, load_sem.at[0])
    load_table = pltpu.make_async_copy(right_in, table, load_sem.at[1])
    load_tiles.start()
    load_table.start()
    own_left = pltpu.make_async_copy(left_in, left.at[cut(r, lw), :], load_sem.at[2])
    own_left.start()
    load_old = pltpu.make_async_copy(old_in, gene_out, load_sem.at[3])

    pl.semaphore_wait(barrier, (n_rank - 1) + len(gene_peers) + (n_cell - 1))

    direct, relay = quarter // 2, quarter // 4
    agz = []
    for i, at in enumerate(
        (cut(g, quarter), pl.ds(pl.multiple_of(gd * quarter, quarter), direct))
    ):
        for k in range(1, n_rank):
            s = i * (n_rank - 1) + k - 1
            copy = remote(
                left_in.at[:, at], left.at[cut(r, lw), at],
                agz_s.at[s], agz_r.at[s], rank=rank_of(k),
            )
            copy.start()
            agz.append(copy)
    load_tiles.wait()
    load_table.wait()
    load_old.start()

    row_blocks = quarter // brows
    group = min(8, gene_blocks)

    def compute(q):
        def fill(i, carry):
            for u in range(group):
                at = i * group + u
                rb = q * row_blocks + at // gene_blocks
                gb = at % gene_blocks
                slot = code[rb * gene_blocks + gb]
                block = tiles[jnp.maximum(slot - 1, 0)]
                dense[cut(rb, brows), cut(gb, bcols)] = jnp.where(slot > 0, block, jnp.zeros_like(block))
            return carry

        lax.fori_loop(0, row_blocks * gene_blocks // group, fill, 0)

        def multiply(h, carry):
            here = pl.ds(pl.multiple_of(q * quarter + h * (quarter // 2), quarter // 2), quarter // 2)
            part[here, :] = jnp.dot(dense[here, :], table[...], preferred_element_type=f32)
            return carry

        lax.fori_loop(0, 2, multiply, 0)

    h0, h1 = pl.ds(0, half), pl.ds(half, half)

    def shard_of(q, z):
        return pl.ds(pl.multiple_of(q * quarter + z * shard, shard), shard)

    def rs1(i, q, h, peer):
        def pack(z, carry):
            one_s[i, cut(z, shard), :], one_ss[i, z] = encode(part[shard_of(q, z), h])
            return carry

        lax.fori_loop(0, n_rank, pack, 0)
        return ship(
            (one_s.at[i], one_r.at[i]), (one_ss.at[i], one_sr.at[i]), rs1_s.at[i], rs1_r.at[i], gene=peer
        )

    def first_hop(i, z):
        return decode(one_r[i, cut(z, shard), :], one_sr[i, z])

    def second_hop(i, z):
        return decode(two_r[i, cut(z, shard), :], two_sr[i, z])

    compute(gd)
    d0 = rs1(0, gd, h0, gx)
    d1 = rs1(1, gd, h1, gy)
    compute(gx)
    o0 = rs1(2, gx, h0, gx)
    compute(gy)
    o1 = rs1(3, gy, h1, gy)
    compute(g)

    order = [rank_of(k) for k in range(1, n_rank)] + [r]
    second = []
    for i, (first, q, h, peer) in enumerate(((d0, gy, h0, gy), (d1, gx, h1, gx))):
        first.wait_recv()
        copies = []
        for j, z in enumerate(order):
            at = cut(z, shard)
            two_s[i, at, :], two_ss[i, z] = encode(part[shard_of(q, z), h] + first_hop(i, z))
            copies.append(
                ship(
                    (two_s.at[i, at, :], two_r.at[i, at, :]), (two_ss.at[i, z], two_sr.at[i, z]),
                    rs2_s.at[i * n_rank + j], rs2_r.at[i * n_rank + j], gene=peer,
                )
            )
        second.append(copies)

    own_left.wait()
    for copy in agz[: n_rank - 1]:
        copy.wait_recv()
    per_share = 0 if n_rank % n_cell else n_rank // n_cell
    lead = n_rank - per_share
    base = (c + 1) * per_share

    def left_piece(j, act):
        z = lax.rem(base + j, n_rank)
        here = left.at[cut(z, lw), cut(g, quarter)]

        @pl.when(z != r)
        def _():
            for i, peer in enumerate((gx, gy)):
                act(remote(here, here, agx_s.at[j, i], agx_r.at[j, i], gene=peer))

    def left_corner(j, act):
        z = lax.rem(base + j, n_rank)

        @pl.when(z != r)
        def _():
            for i, (q, peer) in enumerate(((gy, gx), (gx, gy))):
                start = pl.multiple_of(q * quarter + direct + i * relay, relay)
                here = left.at[cut(z, lw), pl.ds(start, relay)]
                act(remote(here, here, agd_s.at[j, i], agd_r.at[j, i], gene=peer))

    def start(copy):
        copy.start()

    def wait_recv(copy):
        copy.wait_recv()

    def wait_send(copy):
        copy.wait_send()

    for j in range(lead):
        left_piece(j, start)

    o0.wait_recv()
    o1.wait_recv()
    rsz = []
    for j, z in enumerate(order):
        second[0][j].wait_recv()
        second[1][j].wait_recv()
        here = shard_of(g, z)
        part[here, h0] = part[here, h0] + first_hop(2, z) + second_hop(0, z)
        part[here, h1] = part[here, h1] + first_hop(3, z) + second_hop(1, z)
        if j < n_rank - 1:
            z_s[j], z_ss[j] = encode(part[here, :])
            rsz.append(
                ship((z_s.at[j], z_r.at[j]), (z_ss.at[j], z_sr.at[j]), rsz_s.at[j], rsz_r.at[j], rank=z)
            )

    def core_rows_of(k):
        at = cut(cell_of(k), share)

        def multiply(h, carry):
            here = cut(h, half)
            mine = part[cut(g, quarter), here]
            hi = mine.astype(bf16)
            rest = mine - hi.astype(f32)
            mid = rest.astype(bf16)
            low = (rest - mid.astype(f32)).astype(bf16)
            rows_left = left[at, cut(g, quarter)]
            core_part[at, here] = (
                jnp.dot(rows_left, hi, preferred_element_type=f32)
                + jnp.dot(rows_left, mid, preferred_element_type=f32)
                + jnp.dot(rows_left, low, preferred_element_type=f32)
            )
            return carry

        lax.fori_loop(0, 2, multiply, 0)

    own_share = cut(c, share)
    cc = []
    for k in range(1, n_cell):
        core_rows_of(k)
        copy = remote(
            core_part.at[cut(cell_of(k), share), :], core_cell.at[k - 1],
            cc_s.at[k - 1], cc_r.at[k - 1], cell=cell_of(k),
        )
        copy.start()
        cc.append(copy)
    core_rows_of(0)
    for k in range(1, n_cell):
        cc[k - 1].wait_recv()
        core_part[own_share, :] = core_part[own_share, :] + core_cell[k - 1]
    coded = core_code.dtype == jnp.int16

    def pack(x):
        return encode(x) if coded else (x, jnp.ones((1, x.shape[1]), f32))

    def unpack(x, step):
        return decode(x, step) if coded else x

    cg = []
    for i, peer in enumerate(gene_peers):
        src = pl.ds(pl.multiple_of(c * share + peer * core_rows, 8), core_rows)
        cg_c[i], cg_cs[i] = pack(core_part[src, :])
        cg.append(ship((cg_c.at[i], cg_d.at[i]), (cg_cs.at[i], cg_ds.at[i]), cgs_s.at[i], cgs_r.at[i], gene=peer))
    for j in range(lead, n_rank):
        left_piece(j, start)
    for j in range(lead):
        left_piece(j, wait_recv)
        left_corner(j, start)

    own_rows = pl.ds(pl.multiple_of(c * share + g * core_rows, 8), core_rows)
    for i in range(len(gene_peers)):
        cg[i].wait_recv()
        core_part[own_rows, :] = core_part[own_rows, :] + unpack(cg_d[i], cg_ds[i])
    cr = []
    for k in range(1, n_rank):
        cr_c[k - 1], cr_cs[k - 1] = pack(core_part[own_rows, cut(rank_of(k), lanes)])
        cr.append(
            ship(
                (cr_c.at[k - 1], cr_d.at[k - 1]), (cr_cs.at[k - 1], cr_ds.at[k - 1]),
                crs_s.at[k - 1], crs_r.at[k - 1], rank=rank_of(k),
            )
        )

    final = core_part[own_rows, cut(r, lanes)]
    for k in range(1, n_rank):
        cr[k - 1].wait_recv()
        final = final + unpack(cr_d[k - 1], cr_ds[k - 1])
    out_rows = pl.ds(pl.multiple_of(g * core_rows, 8), core_rows)
    core_code[out_rows, cut(r, lanes)], core_step[g, :, cut(r, lanes)] = pack(final)

    def core_piece(z, ssem, rsem, **where):
        piece = core_code.at[out_rows, cut(z, lanes)]
        step = core_step.at[g, :, cut(z, lanes)]
        return ship((piece, piece), (step, step), ssem, rsem, **where)

    ar = [core_piece(r, ar_s.at[k - 1], ar_r.at[k - 1], rank=rank_of(k)) for k in range(1, n_rank)]
    ag = []

    def spread(k):
        for i, peer in enumerate(gene_peers):
            ag.append(core_piece(rank_of(n_rank - k), ag_s.at[k, i], ag_r.at[k, i], gene=peer))

    spread(0)
    for k in range(1, n_rank):
        ar[k - 1].wait_recv()
        spread(k)
    for j in range(lead, n_rank):
        left_piece(j, wait_recv)
        left_corner(j, start)
    for copy in agz[n_rank - 1 :]:
        copy.wait_recv()
    for j in range(lead):
        left_corner(j, wait_recv)

    chunks = dense.shape[1] // GENE_CHUNK

    def gene_copy(k, j):
        return remote(
            gene_send.at[k - 1, :, cut(j, GENE_CHUNK)], gene_recv.at[k - 1, :, cut(j, GENE_CHUNK)],
            gs_s.at[k - 1, j], gs_r.at[k - 1, j], cell=cell_of(k),
        )

    for k in range(1, n_cell):
        peer_rows = cut(cell_of(k), share)

        def send_chunk(j, carry):
            gene_send[k - 1, :, cut(j, GENE_CHUNK)] = jnp.dot(
                left[peer_rows, :], dense[:, cut(j, GENE_CHUNK)], preferred_element_type=f32
            )
            gene_copy(k, j).start()
            return carry

        lax.fori_loop(0, chunks, send_chunk, 0)

    for copy in rsz:
        copy.wait_recv()
    mine = part[shard_of(g, r), :]
    for j in range(n_rank - 1):
        mine = mine + decode(z_r[j], z_sr[j])
    right_out[...] = mine
    load_old.wait()

    for j in range(lead, n_rank):
        left_corner(j, wait_recv)

    def own_chunk(j, carry):
        here = cut(j, GENE_CHUNK)
        gene_out[:, here] = gene_out[:, here] + jnp.dot(
            left[own_share, :], dense[:, here], preferred_element_type=f32
        )
        return carry

    lax.fori_loop(0, chunks, own_chunk, 0)

    for copy in ag:
        copy.wait_recv()
    for i in range(n_gene):
        at = pl.ds(i * core_rows, core_rows)
        core_out[at, :] = unpack(core_code[at, :], core_step[i])

    for k in range(1, n_cell):

        def add_chunk(j, carry):
            gene_copy(k, j).wait_recv()
            here = cut(j, GENE_CHUNK)
            gene_out[:, here] = gene_out[:, here] + gene_recv[k - 1, :, here]
            return carry

        lax.fori_loop(0, chunks, add_chunk, 0)

    for copy in agz + [d0, d1, o0, o1] + second[0] + second[1] + rsz + cc + cg + cr + ar + ag:
        copy.wait_send()
    for j in range(n_rank):
        left_piece(j, wait_send)
        left_corner(j, wait_send)
    for k in range(1, n_cell):

        def drain(j, carry):
            gene_copy(k, j).wait_send()
            return carry

        lax.fori_loop(0, chunks, drain, 0)


def deliver(*refs):
    given, outs, sem = refs[:3], refs[3:6], refs[6]
    copies = [pltpu.make_async_copy(a, b, sem.at[i]) for i, (a, b) in enumerate(zip(given, outs))]
    for copy in copies:
        copy.start()
    for copy in copies:
        copy.wait()


def body(sizes, blocks, block_pos, block_count, test_right, test_left, gene_sketch_old):
    n_cell, n_gene, n_rank = sizes
    f32, bf16, i16 = jnp.float32, jnp.bfloat16, jnp.int16
    tiles = blocks[0, 0]
    slots, brows, bcols = tiles.shape
    genes, width = test_right.shape
    rows, lw = test_left.shape
    left_width = lw * n_rank
    gene_blocks = genes // bcols
    places = (rows // brows) * gene_blocks
    slot_ids = jnp.arange(slots, dtype=jnp.int32)
    hit = (block_pos[0, 0][None, :] == jnp.arange(places, dtype=jnp.int32)[:, None]) & (
        slot_ids < block_count[0, 0]
    )[None, :]
    code = jnp.sum(jnp.where(hit, slot_ids[None, :] + 1, 0), axis=1).astype(jnp.int32)
    quarter, half = rows // n_gene, width // 2
    shard = quarter // n_rank
    share = left_width // n_cell
    core_rows, lanes = share // n_gene, width // n_rank
    chunks = genes // GENE_CHUNK
    dma = pltpu.SemaphoreType.DMA
    vmem = pltpu.VMEM
    z, x = n_rank - 1, n_gene - 1
    wire = f32 if core_rows % 16 else i16

    def pair(*shape):
        return [dma(shape), dma(shape)]

    def both(shape, kind):
        return [vmem(shape, kind), vmem(shape, kind)]

    outs = (
        jax.ShapeDtypeStruct((shard, width), f32),
        jax.ShapeDtypeStruct((share, genes), f32),
        jax.ShapeDtypeStruct((share, width), f32),
    )
    results = pl.pallas_call(
        functools.partial(kernel, sizes),
        out_shape=outs,
        in_specs=[pl.BlockSpec(memory_space=pltpu.SMEM)] + [pl.BlockSpec(memory_space=pltpu.HBM)] * 4,
        out_specs=tuple(pl.BlockSpec(memory_space=pltpu.VMEM) for _ in range(3)),
        scratch_shapes=[
            vmem((slots, brows, bcols), bf16),
            vmem((rows, genes), bf16),
            vmem((genes, width), bf16),
            vmem((left_width, rows), bf16),
            vmem((rows, width), f32),
            *both((4, quarter, half), i16),
            *both((4, n_rank, 1, half), f32),
            *both((2, quarter, half), i16),
            *both((2, n_rank, 1, half), f32),
            *both((z, shard, width), i16),
            *both((z, 1, width), f32),
            vmem((left_width, width), f32),
            vmem((n_cell - 1, share, width), f32),
            *both((x, core_rows, width), wire),
            *both((x, 1, width), f32),
            *both((z, core_rows, lanes), wire),
            *both((z, 1, lanes), f32),
            vmem((share, width), wire),
            vmem((n_gene, 1, width), f32),
            vmem((n_cell - 1, share, genes), f32),
            vmem((n_cell - 1, share, genes), f32),
            dma((4,)),
            *pair(2 * z),
            *pair(n_rank, 2),
            *pair(n_rank, 2),
            *pair(4, 2),
            *pair(2 * n_rank, 2),
            *pair(z, 2),
            *pair(n_cell - 1),
            *pair(x, 2),
            *pair(z, 2),
            *pair(z, 2),
            *pair(n_rank, x, 2),
            *pair(n_cell - 1, chunks),
        ],
        compiler_params=pltpu.CompilerParams(
            collective_id=0, has_side_effects=True, vmem_limit_bytes=56 * 1024 * 1024
        ),
        name="sketch",
    )(code, tiles, test_right, test_left.T, gene_sketch_old)
    return pl.pallas_call(
        deliver,
        out_shape=outs,
        in_specs=[pl.BlockSpec(memory_space=pl.ANY)] * 3,
        out_specs=tuple(pl.BlockSpec(memory_space=pltpu.HBM) for _ in range(3)),
        scratch_shapes=[dma((3,))],
        name="deliver",
    )(*results)


def solution(mesh):
    sizes = tuple(mesh.shape[name] for name in ("cell", "gene", "rank"))
    return jax.shard_map(
        functools.partial(body, sizes),
        mesh=mesh,
        in_specs=(
            P("cell", ("gene", "rank"), None, None, None),
            P("cell", ("gene", "rank"), None),
            P("cell", ("gene", "rank")),
            P(("gene", "rank"), None),
            P("cell", "rank"),
            P("cell", ("gene", "rank")),
        ),
        out_specs=(P(("cell", "gene", "rank"), None), P("cell", ("gene", "rank")), P("cell", None)),
        check_vma=False,
    )
```

```python
import functools

import jax
import jax.numpy as jnp
from jax import lax
from jax.experimental import pallas as pl
from jax.experimental.pallas import tpu as pltpu
from jax.sharding import PartitionSpec as P

MESH = pl.DeviceIdType.MESH
GENE_CHUNK = 1024
TOP = 32767.0


def encode(x):
    peak = jnp.maximum(jnp.max(jnp.abs(x), axis=0, keepdims=True), 1e-30)
    codes = jnp.round(x * (TOP / peak)).astype(jnp.int32).astype(jnp.int16)
    return codes, peak * (1.0 / TOP)


def decode(codes, step):
    return codes.astype(jnp.int32).astype(jnp.float32) * step


class Group:
    def __init__(self, *copies):
        self.copies = copies

    def start(self):
        for copy in self.copies:
            copy.start()
        return self

    def wait_recv(self):
        for copy in self.copies:
            copy.wait_recv()

    def wait_send(self):
        for copy in self.copies:
            copy.wait_send()


def kernel(
    sizes, code, blocks, right_in, left_in, old_in, right_out, gene_out, core_out,
    tiles, dense, table, left, part, one_s, one_r, one_ss, one_sr, two_s, two_r, two_ss, two_sr,
    z_s, z_r, z_ss, z_sr, core_part, core_cell, cg_c, cg_d, cg_cs, cg_ds, cr_c, cr_d, cr_cs, cr_ds,
    core_code, core_step, gene_send, gene_recv,
    load_sem, agz_s, agz_r, agx_s, agx_r, agd_s, agd_r, rs1_s, rs1_r, rs2_s, rs2_r, rsz_s, rsz_r,
    cc_s, cc_r, cgs_s, cgs_r, crs_s, crs_r, ar_s, ar_r, ag_s, ag_r, gs_s, gs_r,
):
    n_cell, n_gene, n_rank = sizes
    f32, bf16 = jnp.float32, jnp.bfloat16
    c, g, r = lax.axis_index("cell"), lax.axis_index("gene"), lax.axis_index("rank")
    b1, b0 = g // 2, g % 2
    gx = 2 * b1 + (1 - b0)
    gy = 2 * (1 - b1) + b0
    gd = 2 * (1 - b1) + (1 - b0)
    gene_peers = [gx, gy, gd]
    rows, width = part.shape
    quarter = rows // n_gene
    shard = quarter // n_rank
    half = width // 2
    lw = left_in.shape[0]
    left_width = left.shape[0]
    brows, bcols = tiles.shape[1], tiles.shape[2]
    gene_blocks = dense.shape[1] // bcols
    share = left_width // n_cell
    core_rows = share // n_gene
    lanes = width // n_rank

    def rank_of(k):
        return lax.rem(r + k, n_rank)

    def cell_of(k):
        return lax.rem(c + k, n_cell)

    def cut(start, step):
        return pl.ds(pl.multiple_of(start * step, step), step)

    def remote(src, dst, ssem, rsem, **where):
        device = (where.get("cell", c), where.get("gene", g), where.get("rank", r))
        return pltpu.make_async_remote_copy(
            src_ref=src, dst_ref=dst, send_sem=ssem, recv_sem=rsem,
            device_id=device, device_id_type=MESH,
        )

    def ship(codes, steps, ssem, rsem, **where):
        return Group(
            remote(*codes, ssem.at[0], rsem.at[0], **where),
            remote(*steps, ssem.at[1], rsem.at[1], **where),
        ).start()

    barrier = pltpu.get_barrier_semaphore()
    for k in range(1, n_rank):
        pl.semaphore_signal(barrier, inc=1, device_id=(c, g, rank_of(k)), device_id_type=MESH)
    for peer in gene_peers:
        pl.semaphore_signal(barrier, inc=1, device_id=(c, peer, r), device_id_type=MESH)
    for k in range(1, n_cell):
        pl.semaphore_signal(barrier, inc=1, device_id=(cell_of(k), g, r), device_id_type=MESH)

    load_tiles = pltpu.make_async_copy(blocks, tiles, load_sem.at[0])
    load_table = pltpu.make_async_copy(right_in, table, load_sem.at[1])
    load_tiles.start()
    load_table.start()
    own_left = pltpu.make_async_copy(left_in, left.at[cut(r, lw), :], load_sem.at[2])
    own_left.start()
    load_old = pltpu.make_async_copy(old_in, gene_out, load_sem.at[3])

    pl.semaphore_wait(barrier, (n_rank - 1) + len(gene_peers) + (n_cell - 1))

    direct, relay = quarter // 2, quarter // 4
    agz = []
    for i, at in enumerate(
        (cut(g, quarter), pl.ds(pl.multiple_of(gd * quarter, quarter), direct))
    ):
        for k in range(1, n_rank):
            s = i * (n_rank - 1) + k - 1
            copy = remote(
                left_in.at[:, at], left.at[cut(r, lw), at],
                agz_s.at[s], agz_r.at[s], rank=rank_of(k),
            )
            copy.start()
            agz.append(copy)
    load_tiles.wait()
    load_table.wait()
    load_old.start()

    row_blocks = quarter // brows
    group = min(8, gene_blocks)

    def compute(q):
        def fill(i, carry):
            for u in range(group):
                at = i * group + u
                rb = q * row_blocks + at // gene_blocks
                gb = at % gene_blocks
                slot = code[rb * gene_blocks + gb]
                block = tiles[jnp.maximum(slot - 1, 0)]
                dense[cut(rb, brows), cut(gb, bcols)] = jnp.where(slot > 0, block, jnp.zeros_like(block))
            return carry

        lax.fori_loop(0, row_blocks * gene_blocks // group, fill, 0)

        def multiply(h, carry):
            here = pl.ds(pl.multiple_of(q * quarter + h * (quarter // 2), quarter // 2), quarter // 2)
            part[here, :] = jnp.dot(dense[here, :], table[...], preferred_element_type=f32)
            return carry

        lax.fori_loop(0, 2, multiply, 0)

    h0, h1 = pl.ds(0, half), pl.ds(half, half)

    def shard_of(q, z):
        return pl.ds(pl.multiple_of(q * quarter + z * shard, shard), shard)

    def rs1(i, q, h, peer):
        def pack(z, carry):
            one_s[i, cut(z, shard), :], one_ss[i, z] = encode(part[shard_of(q, z), h])
            return carry

        lax.fori_loop(0, n_rank, pack, 0)
        return ship(
            (one_s.at[i], one_r.at[i]), (one_ss.at[i], one_sr.at[i]), rs1_s.at[i], rs1_r.at[i], gene=peer
        )

    def first_hop(i, z):
        return decode(one_r[i, cut(z, shard), :], one_sr[i, z])

    def second_hop(i, z):
        return decode(two_r[i, cut(z, shard), :], two_sr[i, z])

    compute(gd)
    d0 = rs1(0, gd, h0, gx)
    d1 = rs1(1, gd, h1, gy)
    compute(gx)
    o0 = rs1(2, gx, h0, gx)
    compute(gy)
    o1 = rs1(3, gy, h1, gy)
    compute(g)

    order = [rank_of(k) for k in range(1, n_rank)] + [r]
    second = []
    for i, (first, q, h, peer) in enumerate(((d0, gy, h0, gy), (d1, gx, h1, gx))):
        first.wait_recv()
        copies = []
        for j, z in enumerate(order):
            at = cut(z, shard)
            two_s[i, at, :], two_ss[i, z] = encode(part[shard_of(q, z), h] + first_hop(i, z))
            copies.append(
                ship(
                    (two_s.at[i, at, :], two_r.at[i, at, :]), (two_ss.at[i, z], two_sr.at[i, z]),
                    rs2_s.at[i * n_rank + j], rs2_r.at[i * n_rank + j], gene=peer,
                )
            )
        second.append(copies)

    own_left.wait()
    for copy in agz[: n_rank - 1]:
        copy.wait_recv()
    per_share = 0 if n_rank % n_cell else n_rank // n_cell
    lead = n_rank - per_share
    base = (c + 1) * per_share

    def left_piece(j, act):
        z = lax.rem(base + j, n_rank)
        here = left.at[cut(z, lw), cut(g, quarter)]

        @pl.when(z != r)
        def _():
            for i, peer in enumerate((gx, gy)):
                act(remote(here, here, agx_s.at[j, i], agx_r.at[j, i], gene=peer))

    def left_corner(j, act):
        z = lax.rem(base + j, n_rank)

        @pl.when(z != r)
        def _():
            for i, (q, peer) in enumerate(((gy, gx), (gx, gy))):
                start = pl.multiple_of(q * quarter + direct + i * relay, relay)
                here = left.at[cut(z, lw), pl.ds(start, relay)]
                act(remote(here, here, agd_s.at[j, i], agd_r.at[j, i], gene=peer))

    def start(copy):
        copy.start()

    def wait_recv(copy):
        copy.wait_recv()

    def wait_send(copy):
        copy.wait_send()

    for j in range(lead):
        left_piece(j, start)

    o0.wait_recv()
    o1.wait_recv()
    rsz = []
    for j, z in enumerate(order):
        second[0][j].wait_recv()
        second[1][j].wait_recv()
        here = shard_of(g, z)
        part[here, h0] = part[here, h0] + first_hop(2, z) + second_hop(0, z)
        part[here, h1] = part[here, h1] + first_hop(3, z) + second_hop(1, z)
        if j < n_rank - 1:
            z_s[j], z_ss[j] = encode(part[here, :])
            rsz.append(
                ship((z_s.at[j], z_r.at[j]), (z_ss.at[j], z_sr.at[j]), rsz_s.at[j], rsz_r.at[j], rank=z)
            )

    def core_rows_of(k):
        at = cut(cell_of(k), share)

        def multiply(h, carry):
            here = cut(h, half)
            mine = part[cut(g, quarter), here]
            hi = mine.astype(bf16)
            rest = mine - hi.astype(f32)
            mid = rest.astype(bf16)
            low = (rest - mid.astype(f32)).astype(bf16)
            rows_left = left[at, cut(g, quarter)]
            core_part[at, here] = (
                jnp.dot(rows_left, hi, preferred_element_type=f32)
                + jnp.dot(rows_left, mid, preferred_element_type=f32)
                + jnp.dot(rows_left, low, preferred_element_type=f32)
            )
            return carry

        lax.fori_loop(0, 2, multiply, 0)

    own_share = cut(c, share)
    cc = []
    for k in range(1, n_cell):
        core_rows_of(k)
        copy = remote(
            core_part.at[cut(cell_of(k), share), :], core_cell.at[k - 1],
            cc_s.at[k - 1], cc_r.at[k - 1], cell=cell_of(k),
        )
        copy.start()
        cc.append(copy)
    core_rows_of(0)
    for k in range(1, n_cell):
        cc[k - 1].wait_recv()
        core_part[own_share, :] = core_part[own_share, :] + core_cell[k - 1]
    coded = core_code.dtype == jnp.int16

    def pack(x):
        return encode(x) if coded else (x, jnp.ones((1, x.shape[1]), f32))

    def unpack(x, step):
        return decode(x, step) if coded else x

    cg = []
    for i, peer in enumerate(gene_peers):
        src = pl.ds(pl.multiple_of(c * share + peer * core_rows, 8), core_rows)
        cg_c[i], cg_cs[i] = pack(core_part[src, :])
        cg.append(ship((cg_c.at[i], cg_d.at[i]), (cg_cs.at[i], cg_ds.at[i]), cgs_s.at[i], cgs_r.at[i], gene=peer))
    for j in range(lead, n_rank):
        left_piece(j, start)
    for j in range(lead):
        left_piece(j, wait_recv)
        left_corner(j, start)

    own_rows = pl.ds(pl.multiple_of(c * share + g * core_rows, 8), core_rows)
    for i in range(len(gene_peers)):
        cg[i].wait_recv()
        core_part[own_rows, :] = core_part[own_rows, :] + unpack(cg_d[i], cg_ds[i])
    cr = []
    for k in range(1, n_rank):
        cr_c[k - 1], cr_cs[k - 1] = pack(core_part[own_rows, cut(rank_of(k), lanes)])
        cr.append(
            ship(
                (cr_c.at[k - 1], cr_d.at[k - 1]), (cr_cs.at[k - 1], cr_ds.at[k - 1]),
                crs_s.at[k - 1], crs_r.at[k - 1], rank=rank_of(k),
            )
        )

    final = core_part[own_rows, cut(r, lanes)]
    for k in range(1, n_rank):
        cr[k - 1].wait_recv()
        final = final + unpack(cr_d[k - 1], cr_ds[k - 1])
    out_rows = pl.ds(pl.multiple_of(g * core_rows, 8), core_rows)
    core_code[out_rows, cut(r, lanes)], core_step[g, :, cut(r, lanes)] = pack(final)

    def core_piece(z, ssem, rsem, **where):
        piece = core_code.at[out_rows, cut(z, lanes)]
        step = core_step.at[g, :, cut(z, lanes)]
        return ship((piece, piece), (step, step), ssem, rsem, **where)

    ar = [core_piece(r, ar_s.at[k - 1], ar_r.at[k - 1], rank=rank_of(k)) for k in range(1, n_rank)]
    ag = []

    def spread(k):
        for i, peer in enumerate(gene_peers):
            ag.append(core_piece(rank_of(n_rank - k), ag_s.at[k, i], ag_r.at[k, i], gene=peer))

    spread(0)
    for k in range(1, n_rank):
        ar[k - 1].wait_recv()
        spread(k)
    for j in range(lead, n_rank):
        left_piece(j, wait_recv)
        left_corner(j, start)
    for copy in agz[n_rank - 1 :]:
        copy.wait_recv()
    for j in range(lead):
        left_corner(j, wait_recv)

    chunks = dense.shape[1] // GENE_CHUNK

    def gene_copy(k, j):
        return remote(
            gene_send.at[k - 1, :, cut(j, GENE_CHUNK)], gene_recv.at[k - 1, :, cut(j, GENE_CHUNK)],
            gs_s.at[k - 1, j], gs_r.at[k - 1, j], cell=cell_of(k),
        )

    for k in range(1, n_cell):
        peer_rows = cut(cell_of(k), share)

        def send_chunk(j, carry):
            gene_send[k - 1, :, cut(j, GENE_CHUNK)] = jnp.dot(
                left[peer_rows, :], dense[:, cut(j, GENE_CHUNK)], preferred_element_type=f32
            )
            gene_copy(k, j).start()
            return carry

        lax.fori_loop(0, chunks, send_chunk, 0)

    for copy in rsz:
        copy.wait_recv()
    mine = part[shard_of(g, r), :]
    for j in range(n_rank - 1):
        mine = mine + decode(z_r[j], z_sr[j])
    right_out[...] = mine
    load_old.wait()

    for j in range(lead, n_rank):
        left_corner(j, wait_recv)

    def own_chunk(j, carry):
        here = cut(j, GENE_CHUNK)
        gene_out[:, here] = gene_out[:, here] + jnp.dot(
            left[own_share, :], dense[:, here], preferred_element_type=f32
        )
        return carry

    lax.fori_loop(0, chunks, own_chunk, 0)

    for copy in ag:
        copy.wait_recv()
    for i in range(n_gene):
        at = pl.ds(i * core_rows, core_rows)
        core_out[at, :] = unpack(core_code[at, :], core_step[i])

    for k in range(1, n_cell):

        def add_chunk(j, carry):
            gene_copy(k, j).wait_recv()
            here = cut(j, GENE_CHUNK)
            gene_out[:, here] = gene_out[:, here] + gene_recv[k - 1, :, here]
            return carry

        lax.fori_loop(0, chunks, add_chunk, 0)

    for copy in agz + [d0, d1, o0, o1] + second[0] + second[1] + rsz + cc + cg + cr + ar + ag:
        copy.wait_send()
    for j in range(n_rank):
        left_piece(j, wait_send)
        left_corner(j, wait_send)
    for k in range(1, n_cell):

        def drain(j, carry):
            gene_copy(k, j).wait_send()
            return carry

        lax.fori_loop(0, chunks, drain, 0)


def body(sizes, blocks, block_pos, block_count, test_right, test_left, gene_sketch_old):
    n_cell, n_gene, n_rank = sizes
    f32, bf16, i16 = jnp.float32, jnp.bfloat16, jnp.int16
    tiles = blocks[0, 0]
    slots, brows, bcols = tiles.shape
    genes, width = test_right.shape
    rows, lw = test_left.shape
    left_width = lw * n_rank
    gene_blocks = genes // bcols
    places = (rows // brows) * gene_blocks
    slot_ids = jnp.arange(slots, dtype=jnp.int32)
    hit = (block_pos[0, 0][None, :] == jnp.arange(places, dtype=jnp.int32)[:, None]) & (
        slot_ids < block_count[0, 0]
    )[None, :]
    code = jnp.sum(jnp.where(hit, slot_ids[None, :] + 1, 0), axis=1).astype(jnp.int32)
    quarter, half = rows // n_gene, width // 2
    shard = quarter // n_rank
    share = left_width // n_cell
    core_rows, lanes = share // n_gene, width // n_rank
    chunks = genes // GENE_CHUNK
    dma = pltpu.SemaphoreType.DMA
    vmem = pltpu.VMEM
    z, x = n_rank - 1, n_gene - 1
    wire = f32 if core_rows % 16 else i16

    def pair(*shape):
        return [dma(shape), dma(shape)]

    def both(shape, kind):
        return [vmem(shape, kind), vmem(shape, kind)]

    outs = (
        jax.ShapeDtypeStruct((shard, width), f32),
        jax.ShapeDtypeStruct((share, genes), f32),
        jax.ShapeDtypeStruct((share, width), f32),
    )
    return pl.pallas_call(
        functools.partial(kernel, sizes),
        out_shape=tuple(pltpu.VMEM(o.shape, o.dtype) for o in outs),
        in_specs=[pl.BlockSpec(memory_space=pltpu.SMEM)] + [pl.BlockSpec(memory_space=pltpu.HBM)] * 4,
        out_specs=tuple(pl.BlockSpec(memory_space=pltpu.VMEM) for _ in range(3)),
        scratch_shapes=[
            vmem((slots, brows, bcols), bf16),
            vmem((rows, genes), bf16),
            vmem((genes, width), bf16),
            vmem((left_width, rows), bf16),
            vmem((rows, width), f32),
            *both((4, quarter, half), i16),
            *both((4, n_rank, 1, half), f32),
            *both((2, quarter, half), i16),
            *both((2, n_rank, 1, half), f32),
            *both((z, shard, width), i16),
            *both((z, 1, width), f32),
            vmem((left_width, width), f32),
            vmem((n_cell - 1, share, width), f32),
            *both((x, core_rows, width), wire),
            *both((x, 1, width), f32),
            *both((z, core_rows, lanes), wire),
            *both((z, 1, lanes), f32),
            vmem((share, width), wire),
            vmem((n_gene, 1, width), f32),
            vmem((n_cell - 1, share, genes), f32),
            vmem((n_cell - 1, share, genes), f32),
            dma((4,)),
            *pair(2 * z),
            *pair(n_rank, 2),
            *pair(n_rank, 2),
            *pair(4, 2),
            *pair(2 * n_rank, 2),
            *pair(z, 2),
            *pair(n_cell - 1),
            *pair(x, 2),
            *pair(z, 2),
            *pair(z, 2),
            *pair(n_rank, x, 2),
            *pair(n_cell - 1, chunks),
        ],
        compiler_params=pltpu.CompilerParams(
            collective_id=0, has_side_effects=True, vmem_limit_bytes=56 * 1024 * 1024
        ),
        name="sketch",
    )(code, tiles, test_right, test_left.T, gene_sketch_old)


def solution(mesh):
    sizes = tuple(mesh.shape[name] for name in ("cell", "gene", "rank"))
    return jax.shard_map(
        functools.partial(body, sizes),
        mesh=mesh,
        in_specs=(
            P("cell", ("gene", "rank"), None, None, None),
            P("cell", ("gene", "rank"), None),
            P("cell", ("gene", "rank")),
            P(("gene", "rank"), None),
            P("cell", "rank"),
            P("cell", ("gene", "rank")),
        ),
        out_specs=(P(("cell", "gene", "rank"), None), P("cell", ("gene", "rank")), P("cell", None)),
        check_vma=False,
    )
```

```python
import functools

import jax
import jax.numpy as jnp
from jax import lax
from jax.experimental import pallas as pl
from jax.experimental.pallas import tpu as pltpu
from jax.sharding import PartitionSpec as P

MESH = pl.DeviceIdType.MESH
GENE_CHUNK = 1024
TOP = 32767.0


def encode(x):
    peak = jnp.maximum(jnp.max(jnp.abs(x), axis=0, keepdims=True), 1e-30)
    codes = jnp.round(x * (TOP / peak)).astype(jnp.int32).astype(jnp.int16)
    return codes, peak * (1.0 / TOP)


def decode(codes, step):
    return codes.astype(jnp.int32).astype(jnp.float32) * step


class Group:
    def __init__(self, *copies):
        self.copies = copies

    def start(self):
        for copy in self.copies:
            copy.start()
        return self

    def wait_recv(self):
        for copy in self.copies:
            copy.wait_recv()

    def wait_send(self):
        for copy in self.copies:
            copy.wait_send()


def kernel(
    sizes, pos, count, blocks, right_in, left_in, old_in, right_out, gene_out, core_out,
    spots, code,
    tiles, dense, table, left, part, one_s, one_r, one_ss, one_sr, two_s, two_r, two_ss, two_sr,
    z_s, z_r, z_ss, z_sr, pieces, core_part, core_cell, cg_c, cg_d, cg_cs, cg_ds, cr_c, cr_d, cr_cs, cr_ds,
    core_code, core_step, gene_send, gene_recv,
    load_sem, agz_s, agz_r, agf_s, agx_s, agx_r, rsd_s, rsd_r, rs1_s, rs1_r, rs2_s, rs2_r, rsz_s, rsz_r,
    cc_s, cc_r, cgs_s, cgs_r, crs_s, crs_r, ar_s, ar_r, ag_s, ag_r, gs_s, gs_r,
):
    n_cell, n_gene, n_rank = sizes
    f32, bf16 = jnp.float32, jnp.bfloat16
    c, g, r = lax.axis_index("cell"), lax.axis_index("gene"), lax.axis_index("rank")
    b1, b0 = g // 2, g % 2
    gx = 2 * b1 + (1 - b0)
    gy = 2 * (1 - b1) + b0
    gd = 2 * (1 - b1) + (1 - b0)
    gene_peers = [gx, gy, gd]
    rows, width = part.shape
    quarter = rows // n_gene
    shard = quarter // n_rank
    half = width // 2
    lw = left_in.shape[0]
    left_width = left.shape[0]
    brows, bcols = tiles.shape[1], tiles.shape[2]
    gene_blocks = dense.shape[1] // bcols
    share = left_width // n_cell
    core_rows = share // n_gene
    lanes = width // n_rank

    def rank_of(k):
        return lax.rem(r + k, n_rank)

    def cell_of(k):
        return lax.rem(c + k, n_cell)

    def cut(start, step):
        return pl.ds(pl.multiple_of(start * step, step), step)

    def remote(src, dst, ssem, rsem, **where):
        device = (where.get("cell", c), where.get("gene", g), where.get("rank", r))
        return pltpu.make_async_remote_copy(
            src_ref=src, dst_ref=dst, send_sem=ssem, recv_sem=rsem,
            device_id=device, device_id_type=MESH,
        )

    def ship(codes, steps, ssem, rsem, **where):
        return Group(
            remote(*codes, ssem.at[0], rsem.at[0], **where),
            remote(*steps, ssem.at[1], rsem.at[1], **where),
        ).start()

    barrier = pltpu.get_barrier_semaphore()
    for k in range(1, n_rank):
        pl.semaphore_signal(barrier, inc=1, device_id=(c, g, rank_of(k)), device_id_type=MESH)
    for peer in gene_peers:
        pl.semaphore_signal(barrier, inc=1, device_id=(c, peer, r), device_id_type=MESH)
    for k in range(1, n_cell):
        pl.semaphore_signal(barrier, inc=1, device_id=(cell_of(k), g, r), device_id_type=MESH)

    load_tiles = pltpu.make_async_copy(blocks, tiles, load_sem.at[0])
    load_table = pltpu.make_async_copy(right_in, table, load_sem.at[1])
    load_tiles.start()
    load_table.start()
    own_left = pltpu.make_async_copy(left_in, left.at[cut(r, lw), :], load_sem.at[2])
    own_left.start()
    def note(s, spot):
        return jnp.where(lax.broadcasted_iota(jnp.int32, spot.shape, 1) == pos[0, 0, s], jnp.where(s < count[0, 0], s + 1, 0), spot)

    spots[...] = lax.fori_loop(0, tiles.shape[0], note, jnp.zeros(spots.shape, jnp.int32), unroll=8)
    load_code = pltpu.make_async_copy(spots, code, load_sem.at[4])
    load_code.start()
    load_old = pltpu.make_async_copy(old_in, gene_out, load_sem.at[3])

    pl.semaphore_wait(barrier, (n_rank - 1) + len(gene_peers) + (n_cell - 1))

    line = n_rank == 4
    quarters = (cut(g, quarter), cut(gd, quarter))

    def rank_piece(i, z, act):
        @pl.when((z != r) & (z - r != 3) & (r - z != 3) if line else z != r)
        def _():
            at = quarters[i]
            act(remote(left_in.at[:, at], left.at[cut(r, lw), at], agz_s.at[i, z], agz_r.at[i, r], rank=z))

    def rank_arrival(i, z):
        here = left.at[cut(z, lw), quarters[i]]
        return remote(here, here, agz_s.at[i, z], agz_r.at[i, z], rank=z)

    def rank_wait(i, z):
        passed = ((r == 2) & (z == 0)) | ((r == 1) & (z == 3)) if line else r < 0

        @pl.when((z != r) & jnp.logical_not(passed))
        def _():
            rank_arrival(i, z).wait_recv()

    def rank_pass(i, act):
        for via, source, target in ((2, 0, 3), (1, 3, 0)) if line else ():

            @pl.when(r == via)
            def _():
                here = left.at[cut(source, lw), quarters[i]]
                act(source, remote(here, here, agf_s.at[i], agz_r.at[i, source], rank=target))

    def pass_on(i):
        def go(source, copy):
            rank_arrival(i, source).wait_recv()
            copy.start()

        rank_pass(i, go)

    def start(copy):
        copy.start()

    def wait_recv(copy):
        copy.wait_recv()

    def wait_send(copy):
        copy.wait_send()

    for z in range(n_rank):
        rank_piece(0, z, start)
    load_tiles.wait()
    load_table.wait()
    load_code.wait()
    load_old.start()

    row_blocks = quarter // brows
    group = min(8, gene_blocks)

    def compute(q):
        def fill(i, carry):
            for u in range(group):
                at = i * group + u
                rb = q * row_blocks + at // gene_blocks
                gb = at % gene_blocks
                slot = code[0, rb * gene_blocks + gb]
                block = tiles[jnp.maximum(slot - 1, 0)]
                dense[cut(rb, brows), cut(gb, bcols)] = jnp.where(slot > 0, block, jnp.zeros_like(block))
            return carry

        lax.fori_loop(0, row_blocks * gene_blocks // group, fill, 0)

        def multiply(h, carry):
            here = pl.ds(pl.multiple_of(q * quarter + h * (quarter // 2), quarter // 2), quarter // 2)
            part[here, :] = jnp.dot(dense[here, :], table[...], preferred_element_type=f32)
            return carry

        lax.fori_loop(0, 2, multiply, 0)

    h0, h1 = pl.ds(0, half), pl.ds(half, half)

    def shard_of(q, z):
        return pl.ds(pl.multiple_of(q * quarter + z * shard, shard), shard)

    order = [rank_of(k) for k in range(1, n_rank)] + [r]

    def rs1_shards(i, q, h, peer):
        copies = []
        for j, z in enumerate(order):
            at = cut(z, shard)
            one_s[i, at, :], one_ss[i, z] = encode(part[shard_of(q, z), h])
            copies.append(
                ship(
                    (one_s.at[i, at, :], one_r.at[i, at, :]), (one_ss.at[i, z], one_sr.at[i, z]),
                    rsd_s.at[i * n_rank + j], rsd_r.at[i * n_rank + j], gene=peer,
                )
            )
        return copies

    def rs1(i, q, h, peer):
        def pack(z, carry):
            one_s[i, cut(z, shard), :], one_ss[i, z] = encode(part[shard_of(q, z), h])
            return carry

        lax.fori_loop(0, n_rank, pack, 0)
        return ship(
            (one_s.at[i], one_r.at[i]), (one_ss.at[i], one_sr.at[i]), rs1_s.at[i - 2], rs1_r.at[i - 2], gene=peer
        )

    def first_hop(i, z):
        return decode(one_r[i, cut(z, shard), :], one_sr[i, z])

    def second_hop(i, z):
        return decode(two_r[i, cut(z, shard), :], two_sr[i, z])

    compute(gd)
    d0 = rs1_shards(0, gd, h0, gx)
    d1 = rs1_shards(1, gd, h1, gy)
    compute(gx)
    o0 = rs1(2, gx, h0, gx)
    compute(gy)
    o1 = rs1(3, gy, h1, gy)
    compute(g)
    for z in range(n_rank):
        rank_piece(1, z, start)

    second = [[], []]
    for j, z in enumerate(order):
        for i, (first, q, h, peer) in enumerate(((d0, gy, h0, gy), (d1, gx, h1, gx))):
            first[j].wait_recv()
            at = cut(z, shard)
            two_s[i, at, :], two_ss[i, z] = encode(part[shard_of(q, z), h] + first_hop(i, z))
            second[i].append(
                ship(
                    (two_s.at[i, at, :], two_r.at[i, at, :]), (two_ss.at[i, z], two_sr.at[i, z]),
                    rs2_s.at[i * n_rank + j], rs2_r.at[i * n_rank + j], gene=peer,
                )
            )

    own_left.wait()
    pass_on(0)
    per_share = 0 if n_rank % n_cell else n_rank // n_cell
    lead = n_rank - per_share
    base = (c + 1) * per_share

    def slice_of(j):
        return lax.rem(base + j, n_rank)

    def left_piece(j, act):
        z = slice_of(j)
        here = left.at[cut(z, lw), cut(g, quarter)]

        @pl.when(z != r)
        def _():
            for i, peer in enumerate((gx, gy)):
                act(remote(here, here, agx_s.at[j, i], agx_r.at[j, i], gene=peer))

    for j in range(lead):
        rank_wait(0, slice_of(j))
        left_piece(j, start)

    o0.wait_recv()
    o1.wait_recv()
    rsz = []
    for j, z in enumerate(order):
        second[0][j].wait_recv()
        second[1][j].wait_recv()
        here = shard_of(g, z)
        part[here, h0] = part[here, h0] + first_hop(2, z) + second_hop(0, z)
        part[here, h1] = part[here, h1] + first_hop(3, z) + second_hop(1, z)
        if j < n_rank - 1:
            z_s[j], z_ss[j] = encode(part[here, :])
            rsz.append(
                ship((z_s.at[j], z_r.at[j]), (z_ss.at[j], z_sr.at[j]), rsz_s.at[j], rsz_r.at[j], rank=z)
            )
        mine = part[here, :]
        high = mine.astype(bf16)
        pieces[0, cut(z, shard), :] = high
        pieces[1, cut(z, shard), :] = (mine - high.astype(f32)).astype(bf16)

    for j in range(lead, n_rank):
        rank_wait(0, slice_of(j))

    def core_rows_of(k):
        at = cut(cell_of(k), share)

        def multiply(h, carry):
            here = cut(h, half)
            rows_left = left[at, cut(g, quarter)]
            core_part[at, here] = jnp.dot(rows_left, pieces[0, :, here], preferred_element_type=f32) + jnp.dot(
                rows_left, pieces[1, :, here], preferred_element_type=f32
            )
            return carry

        lax.fori_loop(0, 2, multiply, 0)

    own_share = cut(c, share)
    cc = []
    for k in range(1, n_cell):
        core_rows_of(k)
        copy = remote(
            core_part.at[cut(cell_of(k), share), :], core_cell.at[k - 1],
            cc_s.at[k - 1], cc_r.at[k - 1], cell=cell_of(k),
        )
        copy.start()
        cc.append(copy)
    core_rows_of(0)
    for k in range(1, n_cell):
        cc[k - 1].wait_recv()
        core_part[own_share, :] = core_part[own_share, :] + core_cell[k - 1]
    coded = core_code.dtype == jnp.int16

    def pack(x):
        return encode(x) if coded else (x, jnp.ones((1, x.shape[1]), f32))

    def unpack(x, step):
        return decode(x, step) if coded else x

    cg = []
    for i, peer in enumerate(gene_peers):
        src = pl.ds(pl.multiple_of(c * share + peer * core_rows, 8), core_rows)
        cg_c[i], cg_cs[i] = pack(core_part[src, :])
        cg.append(ship((cg_c.at[i], cg_d.at[i]), (cg_cs.at[i], cg_ds.at[i]), cgs_s.at[i], cgs_r.at[i], gene=peer))
    for j in range(lead, n_rank):
        left_piece(j, start)
    pass_on(1)

    own_rows = pl.ds(pl.multiple_of(c * share + g * core_rows, 8), core_rows)
    for i in range(len(gene_peers)):
        cg[i].wait_recv()
        core_part[own_rows, :] = core_part[own_rows, :] + unpack(cg_d[i], cg_ds[i])
    cr = []
    for k in range(1, n_rank):
        cr_c[k - 1], cr_cs[k - 1] = pack(core_part[own_rows, cut(rank_of(k), lanes)])
        cr.append(
            ship(
                (cr_c.at[k - 1], cr_d.at[k - 1]), (cr_cs.at[k - 1], cr_ds.at[k - 1]),
                crs_s.at[k - 1], crs_r.at[k - 1], rank=rank_of(k),
            )
        )

    for j in range(lead):
        left_piece(j, wait_recv)
        rank_wait(1, slice_of(j))

    chunks = dense.shape[1] // GENE_CHUNK

    def gene_copy(k, j):
        return remote(
            gene_send.at[k - 1, :, cut(j, GENE_CHUNK)], gene_recv.at[k - 1, :, cut(j, GENE_CHUNK)],
            gs_s.at[k - 1, j], gs_r.at[k - 1, j], cell=cell_of(k),
        )

    for k in range(1, n_cell):
        peer_rows = cut(cell_of(k), share)

        def send_chunk(j, carry):
            gene_send[k - 1, :, cut(j, GENE_CHUNK)] = jnp.dot(
                left[peer_rows, :], dense[:, cut(j, GENE_CHUNK)], preferred_element_type=f32
            )
            gene_copy(k, j).start()
            return carry

        lax.fori_loop(0, chunks, send_chunk, 0)

    final = core_part[own_rows, cut(r, lanes)]
    for k in range(1, n_rank):
        cr[k - 1].wait_recv()
        final = final + unpack(cr_d[k - 1], cr_ds[k - 1])
    out_rows = pl.ds(pl.multiple_of(g * core_rows, 8), core_rows)
    core_code[out_rows, cut(r, lanes)], core_step[g, :, cut(r, lanes)] = pack(final)

    def core_piece(z, ssem, rsem, **where):
        piece = core_code.at[out_rows, cut(z, lanes)]
        step = core_step.at[g, :, cut(z, lanes)]
        return ship((piece, piece), (step, step), ssem, rsem, **where)

    ar = [core_piece(r, ar_s.at[k - 1], ar_r.at[k - 1], rank=rank_of(k)) for k in range(1, n_rank)]
    ag = []

    def spread(k):
        for i, peer in enumerate(gene_peers):
            ag.append(core_piece(rank_of(n_rank - k), ag_s.at[k, i], ag_r.at[k, i], gene=peer))

    spread(0)
    for k in range(1, n_rank):
        ar[k - 1].wait_recv()
        spread(k)
    for copy in rsz:
        copy.wait_recv()
    mine = part[shard_of(g, r), :]
    for j in range(n_rank - 1):
        mine = mine + decode(z_r[j], z_sr[j])
    right_out[...] = mine
    load_old.wait()

    for j in range(lead, n_rank):
        left_piece(j, wait_recv)
        rank_wait(1, slice_of(j))

    def own_chunk(j, carry):
        here = cut(j, GENE_CHUNK)
        gene_out[:, here] = gene_out[:, here] + jnp.dot(
            left[own_share, :], dense[:, here], preferred_element_type=f32
        )
        return carry

    lax.fori_loop(0, chunks, own_chunk, 0)

    for copy in ag:
        copy.wait_recv()
    for i in range(n_gene):
        at = pl.ds(i * core_rows, core_rows)
        core_out[at, :] = unpack(core_code[at, :], core_step[i])

    for k in range(1, n_cell):

        def add_chunk(j, carry):
            gene_copy(k, j).wait_recv()
            here = cut(j, GENE_CHUNK)
            gene_out[:, here] = gene_out[:, here] + gene_recv[k - 1, :, here]
            return carry

        lax.fori_loop(0, chunks, add_chunk, 0)

    for copy in d0 + d1 + [o0, o1] + second[0] + second[1] + rsz + cc + cg + cr + ar + ag:
        copy.wait_send()
    for j in range(n_rank):
        left_piece(j, wait_send)
    for i in range(2):
        for z in range(n_rank):
            rank_piece(i, z, wait_send)
        rank_pass(i, lambda source, copy: copy.wait_send())
    for k in range(1, n_cell):

        def drain(j, carry):
            gene_copy(k, j).wait_send()
            return carry

        lax.fori_loop(0, chunks, drain, 0)


def body(sizes, blocks, block_pos, block_count, test_right, test_left, gene_sketch_old):
    n_cell, n_gene, n_rank = sizes
    f32, bf16, i16 = jnp.float32, jnp.bfloat16, jnp.int16
    tiles = blocks[0, 0]
    slots, brows, bcols = tiles.shape
    genes, width = test_right.shape
    rows, lw = test_left.shape
    left_width = lw * n_rank
    gene_blocks = genes // bcols
    places = (rows // brows) * gene_blocks
    quarter, half = rows // n_gene, width // 2
    shard = quarter // n_rank
    share = left_width // n_cell
    core_rows, lanes = share // n_gene, width // n_rank
    chunks = genes // GENE_CHUNK
    dma = pltpu.SemaphoreType.DMA
    vmem = pltpu.VMEM
    z, x = n_rank - 1, n_gene - 1
    wire = f32 if core_rows % 16 else i16

    def pair(*shape):
        return [dma(shape), dma(shape)]

    def both(shape, kind):
        return [vmem(shape, kind), vmem(shape, kind)]

    outs = (
        jax.ShapeDtypeStruct((shard, width), f32),
        jax.ShapeDtypeStruct((share, genes), f32),
        jax.ShapeDtypeStruct((share, width), f32),
    )
    return pl.pallas_call(
        functools.partial(kernel, sizes),
        out_shape=tuple(pltpu.VMEM(o.shape, o.dtype) for o in outs),
        in_specs=[pl.BlockSpec(memory_space=pltpu.SMEM)] * 2 + [pl.BlockSpec(memory_space=pltpu.HBM)] * 4,
        out_specs=tuple(pl.BlockSpec(memory_space=pltpu.VMEM) for _ in range(3)),
        scratch_shapes=[
            vmem((1, places), jnp.int32),
            pltpu.SMEM((1, places), jnp.int32),
            vmem((slots, brows, bcols), bf16),
            vmem((rows, genes), bf16),
            vmem((genes, width), bf16),
            vmem((left_width, rows), bf16),
            vmem((rows, width), f32),
            *both((4, quarter, half), i16),
            *both((4, n_rank, 1, half), f32),
            *both((2, quarter, half), i16),
            *both((2, n_rank, 1, half), f32),
            *both((z, shard, width), i16),
            *both((z, 1, width), f32),
            vmem((2, quarter, width), bf16),
            vmem((left_width, width), f32),
            vmem((n_cell - 1, share, width), f32),
            *both((x, core_rows, width), wire),
            *both((x, 1, width), f32),
            *both((z, core_rows, lanes), wire),
            *both((z, 1, lanes), f32),
            vmem((share, width), wire),
            vmem((n_gene, 1, width), f32),
            vmem((n_cell - 1, share, genes), f32),
            vmem((n_cell - 1, share, genes), f32),
            dma((5,)),
            *pair(2, n_rank),
            dma((2,)),
            *pair(n_rank, 2),
            *pair(2 * n_rank, 2),
            *pair(2, 2),
            *pair(2 * n_rank, 2),
            *pair(z, 2),
            *pair(n_cell - 1),
            *pair(x, 2),
            *pair(z, 2),
            *pair(z, 2),
            *pair(n_rank, x, 2),
            *pair(n_cell - 1, chunks),
        ],
        compiler_params=pltpu.CompilerParams(
            collective_id=0, has_side_effects=True, vmem_limit_bytes=56 * 1024 * 1024
        ),
        name="sketch",
    )(block_pos, block_count, tiles, test_right, test_left.T, gene_sketch_old)


def solution(mesh):
    sizes = tuple(mesh.shape[name] for name in ("cell", "gene", "rank"))
    return jax.shard_map(
        functools.partial(body, sizes),
        mesh=mesh,
        in_specs=(
            P("cell", ("gene", "rank"), None, None, None),
            P("cell", ("gene", "rank"), None),
            P("cell", ("gene", "rank")),
            P(("gene", "rank"), None),
            P("cell", "rank"),
            P("cell", ("gene", "rank")),
        ),
        out_specs=(P(("cell", "gene", "rank"), None), P("cell", ("gene", "rank")), P("cell", None)),
        check_vma=False,
    )
```

```python
import functools

import jax
import jax.numpy as jnp
from jax import lax
from jax.experimental import pallas as pl
from jax.experimental.pallas import tpu as pltpu
from jax.sharding import PartitionSpec as P

MESH = pl.DeviceIdType.MESH
GENE_CHUNK = 1024
TOP = 32767.0


def encode(x):
    peak = jnp.maximum(jnp.max(jnp.abs(x), axis=0, keepdims=True), 1e-30)
    codes = jnp.round(x * (TOP / peak)).astype(jnp.int32).astype(jnp.int16)
    return codes, peak * (1.0 / TOP)


def decode(codes, step):
    return codes.astype(jnp.int32).astype(jnp.float32) * step


class Group:
    def __init__(self, *copies):
        self.copies = copies

    def start(self):
        for copy in self.copies:
            copy.start()
        return self

    def wait_recv(self):
        for copy in self.copies:
            copy.wait_recv()

    def wait_send(self):
        for copy in self.copies:
            copy.wait_send()


def kernel(
    sizes, pos, count, blocks, right_in, left_in, old_in, right_out, gene_out, core_out,
    spots, code,
    tiles, dense, table, left, part, one_s, one_r, one_ss, one_sr, two_s, two_r, two_ss, two_sr,
    z_s, z_r, z_ss, z_sr, pieces, core_part, core_cell, cg_c, cg_d, cg_cs, cg_ds, cr_c, cr_d, cr_cs, cr_ds,
    core_code, core_step, gene_send, gene_recv,
    load_sem, agz_s, agz_r, agf_s, agx_s, agx_r, rsd_s, rsd_r, rs1_s, rs1_r, rs2_s, rs2_r, rsz_s, rsz_r,
    cc_s, cc_r, cgs_s, cgs_r, crs_s, crs_r, ar_s, ar_r, ag_s, ag_r, gs_s, gs_r,
):
    n_cell, n_gene, n_rank = sizes
    f32, bf16 = jnp.float32, jnp.bfloat16
    c, g, r = lax.axis_index("cell"), lax.axis_index("gene"), lax.axis_index("rank")
    b1, b0 = g // 2, g % 2
    gx = 2 * b1 + (1 - b0)
    gy = 2 * (1 - b1) + b0
    gd = 2 * (1 - b1) + (1 - b0)
    gene_peers = [gx, gy, gd]
    rows, width = part.shape
    quarter = rows // n_gene
    shard = quarter // n_rank
    half = width // 2
    lw = left_in.shape[0]
    left_width = left.shape[0]
    brows, bcols = tiles.shape[1], tiles.shape[2]
    gene_blocks = dense.shape[1] // bcols
    share = left_width // n_cell
    core_rows = share // n_gene
    lanes = width // n_rank

    def rank_of(k):
        return lax.rem(r + k, n_rank)

    def cell_of(k):
        return lax.rem(c + k, n_cell)

    def cut(start, step):
        return pl.ds(pl.multiple_of(start * step, step), step)

    def remote(src, dst, ssem, rsem, **where):
        device = (where.get("cell", c), where.get("gene", g), where.get("rank", r))
        return pltpu.make_async_remote_copy(
            src_ref=src, dst_ref=dst, send_sem=ssem, recv_sem=rsem,
            device_id=device, device_id_type=MESH,
        )

    def ship(codes, steps, ssem, rsem, **where):
        return Group(
            remote(*codes, ssem.at[0], rsem.at[0], **where),
            remote(*steps, ssem.at[1], rsem.at[1], **where),
        ).start()

    barrier = pltpu.get_barrier_semaphore()
    for k in range(1, n_rank):
        pl.semaphore_signal(barrier, inc=1, device_id=(c, g, rank_of(k)), device_id_type=MESH)
    for peer in gene_peers:
        pl.semaphore_signal(barrier, inc=1, device_id=(c, peer, r), device_id_type=MESH)
    for k in range(1, n_cell):
        pl.semaphore_signal(barrier, inc=1, device_id=(cell_of(k), g, r), device_id_type=MESH)

    load_tiles = pltpu.make_async_copy(blocks, tiles, load_sem.at[0])
    load_table = pltpu.make_async_copy(right_in, table, load_sem.at[1])
    load_tiles.start()
    load_table.start()
    own_left = pltpu.make_async_copy(left_in, left.at[cut(r, lw), :], load_sem.at[2])
    def note(s, spot):
        return jnp.where(lax.broadcasted_iota(jnp.int32, spot.shape, 1) == pos[0, 0, s], jnp.where(s < count[0, 0], s + 1, 0), spot)

    spots[...] = lax.fori_loop(0, tiles.shape[0], note, jnp.zeros(spots.shape, jnp.int32), unroll=8)
    load_code = pltpu.make_async_copy(spots, code, load_sem.at[4])
    load_code.start()
    load_old = pltpu.make_async_copy(old_in, gene_out, load_sem.at[3])

    pl.semaphore_wait(barrier, (n_rank - 1) + len(gene_peers) + (n_cell - 1))

    line = n_rank == 4
    quarters = (cut(g, quarter), cut(gd, quarter))

    def rank_pieces(i, act):
        for near in (False, True) if line else (True,):
            for z in range(n_rank):
                rank_piece(i, z, act, near)

    def rank_piece(i, z, act, near):
        if line:
            wanted = (z - r == 1) | (r - z == 1) if near else (z - r == 2) | (r - z == 2)
        else:
            wanted = z != r

        @pl.when(wanted)
        def _():
            at = quarters[i]
            act(remote(left_in.at[:, at], left.at[cut(r, lw), at], agz_s.at[i, z], agz_r.at[i, r], rank=z))

    def rank_arrival(i, z):
        here = left.at[cut(z, lw), quarters[i]]
        return remote(here, here, agz_s.at[i, z], agz_r.at[i, z], rank=z)

    def rank_wait(i, z):
        passed = ((r == 2) & (z == 0)) | ((r == 1) & (z == 3)) if line else r < 0

        @pl.when((z != r) & jnp.logical_not(passed))
        def _():
            rank_arrival(i, z).wait_recv()

    def rank_pass(i, act):
        for via, source, target in ((2, 0, 3), (1, 3, 0)) if line else ():

            @pl.when(r == via)
            def _():
                here = left.at[cut(source, lw), quarters[i]]
                act(source, remote(here, here, agf_s.at[i], agz_r.at[i, source], rank=target))

    def pass_on(i):
        def go(source, copy):
            rank_arrival(i, source).wait_recv()
            copy.start()

        rank_pass(i, go)

    def start(copy):
        copy.start()

    def wait_recv(copy):
        copy.wait_recv()

    def wait_send(copy):
        copy.wait_send()

    rank_pieces(0, start)
    load_tiles.wait()
    load_table.wait()
    load_code.wait()
    own_left.start()
    load_old.start()

    row_blocks = quarter // brows
    group = min(8, gene_blocks)

    def compute(q):
        def fill(i, carry):
            for u in range(group):
                at = i * group + u
                rb = q * row_blocks + at // gene_blocks
                gb = at % gene_blocks
                slot = code[0, rb * gene_blocks + gb]
                block = tiles[jnp.maximum(slot - 1, 0)]
                dense[cut(rb, brows), cut(gb, bcols)] = jnp.where(slot > 0, block, jnp.zeros_like(block))
            return carry

        lax.fori_loop(0, row_blocks * gene_blocks // group, fill, 0)

        def multiply(h, carry):
            here = pl.ds(pl.multiple_of(q * quarter + h * (quarter // 2), quarter // 2), quarter // 2)
            part[here, :] = jnp.dot(dense[here, :], table[...], preferred_element_type=f32)
            return carry

        lax.fori_loop(0, 2, multiply, 0)

    h0, h1 = pl.ds(0, half), pl.ds(half, half)

    def shard_of(q, z):
        return pl.ds(pl.multiple_of(q * quarter + z * shard, shard), shard)

    order = [rank_of(k) for k in range(1, n_rank)] + [r]

    def rs1_shards(i, q, h, peer):
        copies = []
        for j, z in enumerate(order):
            at = cut(z, shard)
            one_s[i, at, :], one_ss[i, z] = encode(part[shard_of(q, z), h])
            copies.append(
                ship(
                    (one_s.at[i, at, :], one_r.at[i, at, :]), (one_ss.at[i, z], one_sr.at[i, z]),
                    rsd_s.at[i * n_rank + j], rsd_r.at[i * n_rank + j], gene=peer,
                )
            )
        return copies

    def rs1(i, q, h, peer):
        def pack(z, carry):
            one_s[i, cut(z, shard), :], one_ss[i, z] = encode(part[shard_of(q, z), h])
            return carry

        lax.fori_loop(0, n_rank, pack, 0)
        return ship(
            (one_s.at[i], one_r.at[i]), (one_ss.at[i], one_sr.at[i]), rs1_s.at[i - 2], rs1_r.at[i - 2], gene=peer
        )

    def first_hop(i, z):
        return decode(one_r[i, cut(z, shard), :], one_sr[i, z])

    def second_hop(i, z):
        return decode(two_r[i, cut(z, shard), :], two_sr[i, z])

    compute(gd)
    d0 = rs1_shards(0, gd, h0, gx)
    d1 = rs1_shards(1, gd, h1, gy)
    compute(gx)
    o0 = rs1(2, gx, h0, gx)
    compute(gy)
    o1 = rs1(3, gy, h1, gy)
    own_left.wait()
    pass_on(0)
    rank_pieces(1, start)

    second = [[], []]
    for j, z in enumerate(order):
        for i, (first, q, h, peer) in enumerate(((d0, gy, h0, gy), (d1, gx, h1, gx))):
            first[j].wait_recv()
            at = cut(z, shard)
            two_s[i, at, :], two_ss[i, z] = encode(part[shard_of(q, z), h] + first_hop(i, z))
            second[i].append(
                ship(
                    (two_s.at[i, at, :], two_r.at[i, at, :]), (two_ss.at[i, z], two_sr.at[i, z]),
                    rs2_s.at[i * n_rank + j], rs2_r.at[i * n_rank + j], gene=peer,
                )
            )

    compute(g)
    per_share = 0 if n_rank % n_cell else n_rank // n_cell
    lead = n_rank - per_share
    base = (c + 1) * per_share

    def slice_of(j):
        return lax.rem(base + j, n_rank)

    def left_piece(j, act):
        z = slice_of(j)
        here = left.at[cut(z, lw), cut(g, quarter)]

        @pl.when(z != r)
        def _():
            for i, peer in enumerate((gx, gy)):
                act(remote(here, here, agx_s.at[j, i], agx_r.at[j, i], gene=peer))

    for j in range(lead):
        rank_wait(0, slice_of(j))
        left_piece(j, start)

    o0.wait_recv()
    o1.wait_recv()
    rsz = []
    for j, z in enumerate(order):
        second[0][j].wait_recv()
        second[1][j].wait_recv()
        here = shard_of(g, z)
        part[here, h0] = part[here, h0] + first_hop(2, z) + second_hop(0, z)
        part[here, h1] = part[here, h1] + first_hop(3, z) + second_hop(1, z)
        if j < n_rank - 1:
            z_s[j], z_ss[j] = encode(part[here, :])
            rsz.append(
                ship((z_s.at[j], z_r.at[j]), (z_ss.at[j], z_sr.at[j]), rsz_s.at[j], rsz_r.at[j], rank=z)
            )
        mine = part[here, :]
        high = mine.astype(bf16)
        pieces[0, cut(z, shard), :] = high
        pieces[1, cut(z, shard), :] = (mine - high.astype(f32)).astype(bf16)

    for j in range(lead, n_rank):
        rank_wait(0, slice_of(j))

    def core_rows_of(k):
        at = cut(cell_of(k), share)

        def multiply(h, carry):
            here = cut(h, half)
            rows_left = left[at, cut(g, quarter)]
            core_part[at, here] = jnp.dot(rows_left, pieces[0, :, here], preferred_element_type=f32) + jnp.dot(
                rows_left, pieces[1, :, here], preferred_element_type=f32
            )
            return carry

        lax.fori_loop(0, 2, multiply, 0)

    own_share = cut(c, share)
    cc = []
    for k in range(1, n_cell):
        core_rows_of(k)
        copy = remote(
            core_part.at[cut(cell_of(k), share), :], core_cell.at[k - 1],
            cc_s.at[k - 1], cc_r.at[k - 1], cell=cell_of(k),
        )
        copy.start()
        cc.append(copy)
    core_rows_of(0)
    for k in range(1, n_cell):
        cc[k - 1].wait_recv()
        core_part[own_share, :] = core_part[own_share, :] + core_cell[k - 1]
    coded = core_code.dtype == jnp.int16

    def pack(x):
        return encode(x) if coded else (x, jnp.ones((1, x.shape[1]), f32))

    def unpack(x, step):
        return decode(x, step) if coded else x

    cg = []
    for i, peer in enumerate(gene_peers):
        src = pl.ds(pl.multiple_of(c * share + peer * core_rows, 8), core_rows)
        cg_c[i], cg_cs[i] = pack(core_part[src, :])
        cg.append(ship((cg_c.at[i], cg_d.at[i]), (cg_cs.at[i], cg_ds.at[i]), cgs_s.at[i], cgs_r.at[i], gene=peer))
    for j in range(lead, n_rank):
        left_piece(j, start)
    pass_on(1)

    own_rows = pl.ds(pl.multiple_of(c * share + g * core_rows, 8), core_rows)
    for i in range(len(gene_peers)):
        cg[i].wait_recv()
        core_part[own_rows, :] = core_part[own_rows, :] + unpack(cg_d[i], cg_ds[i])
    cr = []
    for k in range(1, n_rank):
        cr_c[k - 1], cr_cs[k - 1] = pack(core_part[own_rows, cut(rank_of(k), lanes)])
        cr.append(
            ship(
                (cr_c.at[k - 1], cr_d.at[k - 1]), (cr_cs.at[k - 1], cr_ds.at[k - 1]),
                crs_s.at[k - 1], crs_r.at[k - 1], rank=rank_of(k),
            )
        )

    for j in range(lead):
        left_piece(j, wait_recv)
        rank_wait(1, slice_of(j))

    chunks = dense.shape[1] // GENE_CHUNK

    def gene_copy(k, j):
        return remote(
            gene_send.at[k - 1, :, cut(j, GENE_CHUNK)], gene_recv.at[k - 1, :, cut(j, GENE_CHUNK)],
            gs_s.at[k - 1, j], gs_r.at[k - 1, j], cell=cell_of(k),
        )

    for k in range(1, n_cell):
        peer_rows = cut(cell_of(k), share)

        def send_chunk(j, carry):
            gene_send[k - 1, :, cut(j, GENE_CHUNK)] = jnp.dot(
                left[peer_rows, :], dense[:, cut(j, GENE_CHUNK)], preferred_element_type=f32
            )
            gene_copy(k, j).start()
            return carry

        lax.fori_loop(0, chunks, send_chunk, 0)

    final = core_part[own_rows, cut(r, lanes)]
    for k in range(1, n_rank):
        cr[k - 1].wait_recv()
        final = final + unpack(cr_d[k - 1], cr_ds[k - 1])
    out_rows = pl.ds(pl.multiple_of(g * core_rows, 8), core_rows)
    core_code[out_rows, cut(r, lanes)], core_step[g, :, cut(r, lanes)] = pack(final)

    def core_piece(z, ssem, rsem, **where):
        piece = core_code.at[out_rows, cut(z, lanes)]
        step = core_step.at[g, :, cut(z, lanes)]
        return ship((piece, piece), (step, step), ssem, rsem, **where)

    ar = [core_piece(r, ar_s.at[k - 1], ar_r.at[k - 1], rank=rank_of(k)) for k in range(1, n_rank)]
    ag = []

    def spread(k):
        for i, peer in enumerate(gene_peers):
            ag.append(core_piece(rank_of(n_rank - k), ag_s.at[k, i], ag_r.at[k, i], gene=peer))

    spread(0)
    for k in range(1, n_rank):
        ar[k - 1].wait_recv()
        spread(k)
    for copy in rsz:
        copy.wait_recv()
    mine = part[shard_of(g, r), :]
    for j in range(n_rank - 1):
        mine = mine + decode(z_r[j], z_sr[j])
    right_out[...] = mine
    load_old.wait()

    for j in range(lead, n_rank):
        left_piece(j, wait_recv)
        rank_wait(1, slice_of(j))

    def own_chunk(j, carry):
        here = cut(j, GENE_CHUNK)
        gene_out[:, here] = gene_out[:, here] + jnp.dot(
            left[own_share, :], dense[:, here], preferred_element_type=f32
        )
        return carry

    lax.fori_loop(0, chunks, own_chunk, 0)

    for copy in ag:
        copy.wait_recv()
    for i in range(n_gene):
        at = pl.ds(i * core_rows, core_rows)
        core_out[at, :] = unpack(core_code[at, :], core_step[i])

    for k in range(1, n_cell):

        def add_chunk(j, carry):
            gene_copy(k, j).wait_recv()
            here = cut(j, GENE_CHUNK)
            gene_out[:, here] = gene_out[:, here] + gene_recv[k - 1, :, here]
            return carry

        lax.fori_loop(0, chunks, add_chunk, 0)

    for copy in d0 + d1 + [o0, o1] + second[0] + second[1] + rsz + cc + cg + cr + ar + ag:
        copy.wait_send()
    for j in range(n_rank):
        left_piece(j, wait_send)
    for i in range(2):
        rank_pieces(i, wait_send)
        rank_pass(i, lambda source, copy: copy.wait_send())
    for k in range(1, n_cell):

        def drain(j, carry):
            gene_copy(k, j).wait_send()
            return carry

        lax.fori_loop(0, chunks, drain, 0)


def body(sizes, blocks, block_pos, block_count, test_right, test_left, gene_sketch_old):
    n_cell, n_gene, n_rank = sizes
    f32, bf16, i16 = jnp.float32, jnp.bfloat16, jnp.int16
    tiles = blocks[0, 0]
    slots, brows, bcols = tiles.shape
    genes, width = test_right.shape
    rows, lw = test_left.shape
    left_width = lw * n_rank
    gene_blocks = genes // bcols
    places = (rows // brows) * gene_blocks
    quarter, half = rows // n_gene, width // 2
    shard = quarter // n_rank
    share = left_width // n_cell
    core_rows, lanes = share // n_gene, width // n_rank
    chunks = genes // GENE_CHUNK
    dma = pltpu.SemaphoreType.DMA
    vmem = pltpu.VMEM
    z, x = n_rank - 1, n_gene - 1
    wire = f32 if core_rows % 16 else i16

    def pair(*shape):
        return [dma(shape), dma(shape)]

    def both(shape, kind):
        return [vmem(shape, kind), vmem(shape, kind)]

    outs = (
        jax.ShapeDtypeStruct((shard, width), f32),
        jax.ShapeDtypeStruct((share, genes), f32),
        jax.ShapeDtypeStruct((share, width), f32),
    )
    return pl.pallas_call(
        functools.partial(kernel, sizes),
        out_shape=tuple(pltpu.VMEM(o.shape, o.dtype) for o in outs),
        in_specs=[pl.BlockSpec(memory_space=pltpu.SMEM)] * 2 + [pl.BlockSpec(memory_space=pltpu.HBM)] * 4,
        out_specs=tuple(pl.BlockSpec(memory_space=pltpu.VMEM) for _ in range(3)),
        scratch_shapes=[
            vmem((1, places), jnp.int32),
            pltpu.SMEM((1, places), jnp.int32),
            vmem((slots, brows, bcols), bf16),
            vmem((rows, genes), bf16),
            vmem((genes, width), bf16),
            vmem((left_width, rows), bf16),
            vmem((rows, width), f32),
            *both((4, quarter, half), i16),
            *both((4, n_rank, 1, half), f32),
            *both((2, quarter, half), i16),
            *both((2, n_rank, 1, half), f32),
            *both((z, shard, width), i16),
            *both((z, 1, width), f32),
            vmem((2, quarter, width), bf16),
            vmem((left_width, width), f32),
            vmem((n_cell - 1, share, width), f32),
            *both((x, core_rows, width), wire),
            *both((x, 1, width), f32),
            *both((z, core_rows, lanes), wire),
            *both((z, 1, lanes), f32),
            vmem((share, width), wire),
            vmem((n_gene, 1, width), f32),
            vmem((n_cell - 1, share, genes), f32),
            vmem((n_cell - 1, share, genes), f32),
            dma((5,)),
            *pair(2, n_rank),
            dma((2,)),
            *pair(n_rank, 2),
            *pair(2 * n_rank, 2),
            *pair(2, 2),
            *pair(2 * n_rank, 2),
            *pair(z, 2),
            *pair(n_cell - 1),
            *pair(x, 2),
            *pair(z, 2),
            *pair(z, 2),
            *pair(n_rank, x, 2),
            *pair(n_cell - 1, chunks),
        ],
        compiler_params=pltpu.CompilerParams(
            collective_id=0, has_side_effects=True, vmem_limit_bytes=56 * 1024 * 1024
        ),
        name="sketch",
    )(block_pos, block_count, tiles, test_right, test_left.T, gene_sketch_old)


def solution(mesh):
    sizes = tuple(mesh.shape[name] for name in ("cell", "gene", "rank"))
    return jax.shard_map(
        functools.partial(body, sizes),
        mesh=mesh,
        in_specs=(
            P("cell", ("gene", "rank"), None, None, None),
            P("cell", ("gene", "rank"), None),
            P("cell", ("gene", "rank")),
            P(("gene", "rank"), None),
            P("cell", "rank"),
            P("cell", ("gene", "rank")),
        ),
        out_specs=(P(("cell", "gene", "rank"), None), P("cell", ("gene", "rank")), P("cell", None)),
        check_vma=False,
    )
```

```python
import functools

import jax
import jax.numpy as jnp
from jax import lax
from jax.experimental import pallas as pl
from jax.experimental.pallas import tpu as pltpu
from jax.sharding import PartitionSpec as P

MESH = pl.DeviceIdType.MESH
GENE_CHUNK = 1024
TOP = 32767.0


def encode(x):
    peak = jnp.maximum(jnp.max(jnp.abs(x), axis=0, keepdims=True), 1e-30)
    codes = jnp.round(x * (TOP / peak)).astype(jnp.int32).astype(jnp.int16)
    return codes, peak * (1.0 / TOP)


def decode(codes, step):
    return codes.astype(jnp.int32).astype(jnp.float32) * step


class Group:
    def __init__(self, *copies):
        self.copies = copies

    def start(self):
        for copy in self.copies:
            copy.start()
        return self

    def wait_recv(self):
        for copy in self.copies:
            copy.wait_recv()

    def wait_send(self):
        for copy in self.copies:
            copy.wait_send()


def kernel(
    sizes, pos, count, blocks, right_in, left_in, old_in, right_out, gene_out, core_out,
    spots, code,
    tiles, dense, table, left, part, one_s, one_r, one_ss, one_sr, two_s, two_r, two_ss, two_sr,
    z_s, z_r, z_ss, z_sr, pieces, core_part, core_cell, cg_c, cg_d, cg_cs, cg_ds, cr_c, cr_d, cr_cs, cr_ds,
    core_code, core_step, gene_send, gene_recv,
    load_sem, agz_s, agz_r, agf_s, agx_s, agx_r, agd_s, agd_r, rsd_s, rsd_r, rs1_s, rs1_r, rs2_s, rs2_r, rsz_s, rsz_r,
    cc_s, cc_r, cgs_s, cgs_r, crs_s, crs_r, ar_s, ar_r, ag_s, ag_r, gs_s, gs_r,
):
    n_cell, n_gene, n_rank = sizes
    f32, bf16 = jnp.float32, jnp.bfloat16
    c, g, r = lax.axis_index("cell"), lax.axis_index("gene"), lax.axis_index("rank")
    b1, b0 = g // 2, g % 2
    gx = 2 * b1 + (1 - b0)
    gy = 2 * (1 - b1) + b0
    gd = 2 * (1 - b1) + (1 - b0)
    gene_peers = [gx, gy, gd]
    rows, width = part.shape
    quarter = rows // n_gene
    shard = quarter // n_rank
    half = width // 2
    lw = left_in.shape[0]
    left_width = left.shape[0]
    brows, bcols = tiles.shape[1], tiles.shape[2]
    gene_blocks = dense.shape[1] // bcols
    share = left_width // n_cell
    core_rows = share // n_gene
    lanes = width // n_rank

    def rank_of(k):
        return lax.rem(r + k, n_rank)

    def cell_of(k):
        return lax.rem(c + k, n_cell)

    def cut(start, step):
        return pl.ds(pl.multiple_of(start * step, step), step)

    def remote(src, dst, ssem, rsem, **where):
        device = (where.get("cell", c), where.get("gene", g), where.get("rank", r))
        return pltpu.make_async_remote_copy(
            src_ref=src, dst_ref=dst, send_sem=ssem, recv_sem=rsem,
            device_id=device, device_id_type=MESH,
        )

    def ship(codes, steps, ssem, rsem, **where):
        return Group(
            remote(*codes, ssem.at[0], rsem.at[0], **where),
            remote(*steps, ssem.at[1], rsem.at[1], **where),
        ).start()

    barrier = pltpu.get_barrier_semaphore()
    for k in range(1, n_rank):
        pl.semaphore_signal(barrier, inc=1, device_id=(c, g, rank_of(k)), device_id_type=MESH)
    for peer in gene_peers:
        pl.semaphore_signal(barrier, inc=1, device_id=(c, peer, r), device_id_type=MESH)
    for k in range(1, n_cell):
        pl.semaphore_signal(barrier, inc=1, device_id=(cell_of(k), g, r), device_id_type=MESH)

    load_tiles = pltpu.make_async_copy(blocks, tiles, load_sem.at[0])
    load_table = pltpu.make_async_copy(right_in, table, load_sem.at[1])
    load_tiles.start()
    load_table.start()
    own_left = pltpu.make_async_copy(left_in, left.at[cut(r, lw), :], load_sem.at[2])
    def note(s, spot):
        return jnp.where(lax.broadcasted_iota(jnp.int32, spot.shape, 1) == pos[0, 0, s], jnp.where(s < count[0, 0], s + 1, 0), spot)

    spots[...] = lax.fori_loop(0, tiles.shape[0], note, jnp.zeros(spots.shape, jnp.int32), unroll=8)
    load_code = pltpu.make_async_copy(spots, code, load_sem.at[4])
    load_code.start()
    load_old = pltpu.make_async_copy(old_in, gene_out, load_sem.at[3])

    pl.semaphore_wait(barrier, (n_rank - 1) + len(gene_peers) + (n_cell - 1))

    line = n_rank == 4
    direct = quarter // 2
    relay = (quarter - direct) // 2
    quarters = (cut(g, quarter), pl.ds(pl.multiple_of(gd * quarter, quarter), direct))

    def rank_pieces(i, act):
        for near in (False, True) if line else (True,):
            for z in range(n_rank):
                rank_piece(i, z, act, near)

    def rank_piece(i, z, act, near):
        if line:
            wanted = (z - r == 1) | (r - z == 1) if near else (z - r == 2) | (r - z == 2)
        else:
            wanted = z != r

        @pl.when(wanted)
        def _():
            at = quarters[i]
            act(remote(left_in.at[:, at], left.at[cut(r, lw), at], agz_s.at[i, z], agz_r.at[i, r], rank=z))

    def rank_arrival(i, z):
        here = left.at[cut(z, lw), quarters[i]]
        return remote(here, here, agz_s.at[i, z], agz_r.at[i, z], rank=z)

    def rank_wait(i, z):
        passed = ((r == 2) & (z == 0)) | ((r == 1) & (z == 3)) if line else r < 0

        @pl.when((z != r) & jnp.logical_not(passed))
        def _():
            rank_arrival(i, z).wait_recv()

    def rank_pass(i, act):
        for via, source, target in ((2, 0, 3), (1, 3, 0)) if line else ():

            @pl.when(r == via)
            def _():
                here = left.at[cut(source, lw), quarters[i]]
                act(source, remote(here, here, agf_s.at[i], agz_r.at[i, source], rank=target))

    def pass_on(i):
        def go(source, copy):
            rank_arrival(i, source).wait_recv()
            copy.start()

        rank_pass(i, go)

    def start(copy):
        copy.start()

    def wait_recv(copy):
        copy.wait_recv()

    def wait_send(copy):
        copy.wait_send()

    rank_pieces(0, start)
    load_tiles.wait()
    load_table.wait()
    load_code.wait()
    own_left.start()
    load_old.start()

    row_blocks = quarter // brows
    group = min(8, gene_blocks)

    def compute(q, first=0, last=2):
        def fill(i, carry):
            for u in range(group):
                at = i * group + u
                rb = q * row_blocks + at // gene_blocks
                gb = at % gene_blocks
                slot = code[0, rb * gene_blocks + gb]
                block = tiles[jnp.maximum(slot - 1, 0)]
                dense[cut(rb, brows), cut(gb, bcols)] = jnp.where(slot > 0, block, jnp.zeros_like(block))
            return carry

        steps = row_blocks * gene_blocks // group // 2
        lax.fori_loop(first * steps, last * steps, fill, 0)

        def multiply(h, carry):
            here = pl.ds(pl.multiple_of(q * quarter + h * (quarter // 2), quarter // 2), quarter // 2)
            part[here, :] = jnp.dot(dense[here, :], table[...], preferred_element_type=f32)
            return carry

        lax.fori_loop(first, last, multiply, 0)

    h0, h1 = pl.ds(0, half), pl.ds(half, half)

    def shard_of(q, z):
        return pl.ds(pl.multiple_of(q * quarter + z * shard, shard), shard)

    order = [rank_of(k) for k in range(1, n_rank)] + [r]

    def rs1_shards(i, q, h, peer, some):
        copies = []
        for z in some:
            j = z
            at = cut(z, shard)
            one_s[i, at, :], one_ss[i, z] = encode(part[shard_of(q, z), h])
            copies.append(
                ship(
                    (one_s.at[i, at, :], one_r.at[i, at, :]), (one_ss.at[i, z], one_sr.at[i, z]),
                    rsd_s.at[i * n_rank + j], rsd_r.at[i * n_rank + j], gene=peer,
                )
            )
        return copies

    def rs1(i, q, h, peer):
        def pack(z, carry):
            one_s[i, cut(z, shard), :], one_ss[i, z] = encode(part[shard_of(q, z), h])
            return carry

        lax.fori_loop(0, n_rank, pack, 0)
        return ship(
            (one_s.at[i], one_r.at[i]), (one_ss.at[i], one_sr.at[i]), rs1_s.at[i - 2], rs1_r.at[i - 2], gene=peer
        )

    def first_hop(i, z):
        return decode(one_r[i, cut(z, shard), :], one_sr[i, z])

    def second_hop(i, z):
        return decode(two_r[i, cut(z, shard), :], two_sr[i, z])

    d0, d1 = [], []
    middle = n_rank // 2
    for at, some in enumerate((range(middle), range(middle, n_rank))):
        compute(gd, at, at + 1)
        d0 += rs1_shards(0, gd, h0, gx, some)
        d1 += rs1_shards(1, gd, h1, gy, some)
    compute(gx)
    o0 = rs1(2, gx, h0, gx)
    compute(gy)
    o1 = rs1(3, gy, h1, gy)
    own_left.wait()
    pass_on(0)
    rank_pieces(1, start)

    second = [[], []]
    for z in range(n_rank):
        for i, (first, q, h, peer) in enumerate(((d0, gy, h0, gy), (d1, gx, h1, gx))):
            first[z].wait_recv()
            at = cut(z, shard)
            two_s[i, at, :], two_ss[i, z] = encode(part[shard_of(q, z), h] + first_hop(i, z))
            second[i].append(
                ship(
                    (two_s.at[i, at, :], two_r.at[i, at, :]), (two_ss.at[i, z], two_sr.at[i, z]),
                    rs2_s.at[i * n_rank + z], rs2_r.at[i * n_rank + z], gene=peer,
                )
            )

    compute(g)
    per_share = 0 if n_rank % n_cell else n_rank // n_cell
    lead = n_rank - per_share
    base = (c + 1) * per_share

    def slice_of(j):
        return lax.rem(base + j, n_rank)

    def left_piece(j, act):
        z = slice_of(j)
        here = left.at[cut(z, lw), cut(g, quarter)]

        @pl.when(z != r)
        def _():
            for i, peer in enumerate((gx, gy)):
                act(remote(here, here, agx_s.at[j, i], agx_r.at[j, i], gene=peer))

    def left_corner(j, act):
        z = slice_of(j)

        @pl.when(z != r)
        def _():
            for i, (q, peer) in enumerate(((gy, gx), (gx, gy))):
                here = left.at[cut(z, lw), pl.ds(pl.multiple_of(q * quarter + direct + i * relay, relay), relay)]
                act(remote(here, here, agd_s.at[j, i], agd_r.at[j, i], gene=peer))

    for j in range(lead):
        rank_wait(0, slice_of(j))
        left_piece(j, start)

    o0.wait_recv()
    o1.wait_recv()
    rsz = []
    for copy in second[0] + second[1]:
        copy.wait_recv()
    for j, z in enumerate(order):
        here = shard_of(g, z)
        part[here, h0] = part[here, h0] + first_hop(2, z) + second_hop(0, z)
        part[here, h1] = part[here, h1] + first_hop(3, z) + second_hop(1, z)
        if j < n_rank - 1:
            z_s[j], z_ss[j] = encode(part[here, :])
            rsz.append(
                ship((z_s.at[j], z_r.at[j]), (z_ss.at[j], z_sr.at[j]), rsz_s.at[j], rsz_r.at[j], rank=z)
            )
        mine = part[here, :]
        high = mine.astype(bf16)
        pieces[0, cut(z, shard), :] = high
        pieces[1, cut(z, shard), :] = (mine - high.astype(f32)).astype(bf16)

    for j in range(lead, n_rank):
        rank_wait(0, slice_of(j))

    def core_rows_of(k):
        at = cut(cell_of(k), share)

        def multiply(h, carry):
            here = cut(h, half)
            rows_left = left[at, cut(g, quarter)]
            core_part[at, here] = jnp.dot(rows_left, pieces[0, :, here], preferred_element_type=f32) + jnp.dot(
                rows_left, pieces[1, :, here], preferred_element_type=f32
            )
            return carry

        lax.fori_loop(0, 2, multiply, 0)

    own_share = cut(c, share)
    cc = []
    for k in range(1, n_cell):
        core_rows_of(k)
        copy = remote(
            core_part.at[cut(cell_of(k), share), :], core_cell.at[k - 1],
            cc_s.at[k - 1], cc_r.at[k - 1], cell=cell_of(k),
        )
        copy.start()
        cc.append(copy)
    core_rows_of(0)
    for k in range(1, n_cell):
        cc[k - 1].wait_recv()
        core_part[own_share, :] = core_part[own_share, :] + core_cell[k - 1]
    coded = core_code.dtype == jnp.int16

    def pack(x):
        return encode(x) if coded else (x, jnp.ones((1, x.shape[1]), f32))

    def unpack(x, step):
        return decode(x, step) if coded else x

    cg = []
    for i, peer in reversed(list(enumerate(gene_peers))):
        src = pl.ds(pl.multiple_of(c * share + peer * core_rows, 8), core_rows)
        cg_c[i], cg_cs[i] = pack(core_part[src, :])
        cg.append(ship((cg_c.at[i], cg_d.at[i]), (cg_cs.at[i], cg_ds.at[i]), cgs_s.at[i], cgs_r.at[i], gene=peer))
    for j in range(lead, n_rank):
        left_piece(j, start)
    pass_on(1)

    own_rows = pl.ds(pl.multiple_of(c * share + g * core_rows, 8), core_rows)
    for i in range(len(gene_peers)):
        cg[-1 - i].wait_recv()
        core_part[own_rows, :] = core_part[own_rows, :] + unpack(cg_d[i], cg_ds[i])
    cr = []
    for k in range(1, n_rank):
        cr_c[k - 1], cr_cs[k - 1] = pack(core_part[own_rows, cut(rank_of(k), lanes)])
        cr.append(
            ship(
                (cr_c.at[k - 1], cr_d.at[k - 1]), (cr_cs.at[k - 1], cr_ds.at[k - 1]),
                crs_s.at[k - 1], crs_r.at[k - 1], rank=rank_of(k),
            )
        )

    for j in range(lead):
        left_piece(j, wait_recv)
        left_corner(j, start)

    final = core_part[own_rows, cut(r, lanes)]
    for k in range(1, n_rank):
        cr[k - 1].wait_recv()
        final = final + unpack(cr_d[k - 1], cr_ds[k - 1])
    out_rows = pl.ds(pl.multiple_of(g * core_rows, 8), core_rows)
    core_code[out_rows, cut(r, lanes)], core_step[g, :, cut(r, lanes)] = pack(final)

    def core_piece(z, ssem, rsem, **where):
        piece = core_code.at[out_rows, cut(z, lanes)]
        step = core_step.at[g, :, cut(z, lanes)]
        return ship((piece, piece), (step, step), ssem, rsem, **where)

    ar = [core_piece(r, ar_s.at[k - 1], ar_r.at[k - 1], rank=rank_of(k)) for k in range(1, n_rank)]
    ag = []

    def spread(k):
        for i, peer in reversed(list(enumerate(gene_peers))):
            ag.append(core_piece(rank_of(n_rank - k), ag_s.at[k, i], ag_r.at[k, i], gene=peer))

    spread(0)
    for j in range(lead, n_rank):
        left_piece(j, wait_recv)
        left_corner(j, start)
    for j in range(lead):
        rank_wait(1, slice_of(j))
        left_corner(j, wait_recv)

    chunks = dense.shape[1] // GENE_CHUNK

    def gene_copy(k, j):
        return remote(
            gene_send.at[k - 1, :, cut(j, GENE_CHUNK)], gene_recv.at[k - 1, :, cut(j, GENE_CHUNK)],
            gs_s.at[k - 1, j], gs_r.at[k - 1, j], cell=cell_of(k),
        )

    for k in range(1, n_cell):
        peer_rows = cut(cell_of(k), share)

        def send_chunk(j, carry):
            gene_send[k - 1, :, cut(j, GENE_CHUNK)] = jnp.dot(
                left[peer_rows, :], dense[:, cut(j, GENE_CHUNK)], preferred_element_type=f32
            )
            gene_copy(k, j).start()
            return carry

        lax.fori_loop(0, chunks, send_chunk, 0)

    for k in range(1, n_rank):
        ar[k - 1].wait_recv()
        spread(k)
    for copy in rsz:
        copy.wait_recv()
    mine = part[shard_of(g, r), :]
    for j in range(n_rank - 1):
        mine = mine + decode(z_r[j], z_sr[j])
    right_out[...] = mine
    load_old.wait()

    for j in range(lead, n_rank):
        rank_wait(1, slice_of(j))
        left_corner(j, wait_recv)

    def own_chunk(j, carry):
        here = cut(j, GENE_CHUNK)
        gene_out[:, here] = gene_out[:, here] + jnp.dot(
            left[own_share, :], dense[:, here], preferred_element_type=f32
        )
        return carry

    lax.fori_loop(0, chunks, own_chunk, 0)

    for copy in ag:
        copy.wait_recv()
    for i in range(n_gene):
        at = pl.ds(i * core_rows, core_rows)
        core_out[at, :] = unpack(core_code[at, :], core_step[i])

    for k in range(1, n_cell):

        def add_chunk(j, carry):
            gene_copy(k, j).wait_recv()
            here = cut(j, GENE_CHUNK)
            gene_out[:, here] = gene_out[:, here] + gene_recv[k - 1, :, here]
            return carry

        lax.fori_loop(0, chunks, add_chunk, 0)

    for copy in d0 + d1 + [o0, o1] + second[0] + second[1] + rsz + cc + cg + cr + ar + ag:
        copy.wait_send()
    for j in range(n_rank):
        left_piece(j, wait_send)
        left_corner(j, wait_send)
    for i in range(2):
        rank_pieces(i, wait_send)
        rank_pass(i, lambda source, copy: copy.wait_send())
    for k in range(1, n_cell):

        def drain(j, carry):
            gene_copy(k, j).wait_send()
            return carry

        lax.fori_loop(0, chunks, drain, 0)


def body(sizes, blocks, block_pos, block_count, test_right, test_left, gene_sketch_old):
    n_cell, n_gene, n_rank = sizes
    f32, bf16, i16 = jnp.float32, jnp.bfloat16, jnp.int16
    tiles = blocks[0, 0]
    slots, brows, bcols = tiles.shape
    genes, width = test_right.shape
    rows, lw = test_left.shape
    left_width = lw * n_rank
    gene_blocks = genes // bcols
    places = (rows // brows) * gene_blocks
    quarter, half = rows // n_gene, width // 2
    shard = quarter // n_rank
    share = left_width // n_cell
    core_rows, lanes = share // n_gene, width // n_rank
    chunks = genes // GENE_CHUNK
    dma = pltpu.SemaphoreType.DMA
    vmem = pltpu.VMEM
    z, x = n_rank - 1, n_gene - 1
    wire = f32 if core_rows % 16 else i16

    def pair(*shape):
        return [dma(shape), dma(shape)]

    def both(shape, kind):
        return [vmem(shape, kind), vmem(shape, kind)]

    outs = (
        jax.ShapeDtypeStruct((shard, width), f32),
        jax.ShapeDtypeStruct((share, genes), f32),
        jax.ShapeDtypeStruct((share, width), f32),
    )
    return pl.pallas_call(
        functools.partial(kernel, sizes),
        out_shape=tuple(pltpu.VMEM(o.shape, o.dtype) for o in outs),
        in_specs=[pl.BlockSpec(memory_space=pltpu.SMEM)] * 2 + [pl.BlockSpec(memory_space=pltpu.HBM)] * 4,
        out_specs=tuple(pl.BlockSpec(memory_space=pltpu.VMEM) for _ in range(3)),
        scratch_shapes=[
            vmem((1, places), jnp.int32),
            pltpu.SMEM((1, places), jnp.int32),
            vmem((slots, brows, bcols), bf16),
            vmem((rows, genes), bf16),
            vmem((genes, width), bf16),
            vmem((left_width, rows), bf16),
            vmem((rows, width), f32),
            *both((4, quarter, half), i16),
            *both((4, n_rank, 1, half), f32),
            *both((2, quarter, half), i16),
            *both((2, n_rank, 1, half), f32),
            *both((z, shard, width), i16),
            *both((z, 1, width), f32),
            vmem((2, quarter, width), bf16),
            vmem((left_width, width), f32),
            vmem((n_cell - 1, share, width), f32),
            *both((x, core_rows, width), wire),
            *both((x, 1, width), f32),
            *both((z, core_rows, lanes), wire),
            *both((z, 1, lanes), f32),
            vmem((share, width), wire),
            vmem((n_gene, 1, width), f32),
            vmem((n_cell - 1, share, genes), f32),
            vmem((n_cell - 1, share, genes), f32),
            dma((5,)),
            *pair(2, n_rank),
            dma((2,)),
            *pair(n_rank, 2),
            *pair(n_rank, 2),
            *pair(2 * n_rank, 2),
            *pair(2, 2),
            *pair(2 * n_rank, 2),
            *pair(z, 2),
            *pair(n_cell - 1),
            *pair(x, 2),
            *pair(z, 2),
            *pair(z, 2),
            *pair(n_rank, x, 2),
            *pair(n_cell - 1, chunks),
        ],
        compiler_params=pltpu.CompilerParams(
            collective_id=0, has_side_effects=True, vmem_limit_bytes=56 * 1024 * 1024
        ),
        name="sketch",
    )(block_pos, block_count, tiles, test_right, test_left.T, gene_sketch_old)


def solution(mesh):
    sizes = tuple(mesh.shape[name] for name in ("cell", "gene", "rank"))
    return jax.shard_map(
        functools.partial(body, sizes),
        mesh=mesh,
        in_specs=(
            P("cell", ("gene", "rank"), None, None, None),
            P("cell", ("gene", "rank"), None),
            P("cell", ("gene", "rank")),
            P(("gene", "rank"), None),
            P("cell", "rank"),
            P("cell", ("gene", "rank")),
        ),
        out_specs=(P(("cell", "gene", "rank"), None), P("cell", ("gene", "rank")), P("cell", None)),
        check_vma=False,
    )
```

```python
import functools

import jax
import jax.numpy as jnp
from jax import lax
from jax.experimental import pallas as pl
from jax.experimental.pallas import tpu as pltpu
from jax.sharding import PartitionSpec as P

MESH = pl.DeviceIdType.MESH
GENE_CHUNK = 1024
TOP = 32767.0


def encode(x):
    peak = jnp.maximum(jnp.max(jnp.abs(x), axis=0, keepdims=True), 1e-30)
    codes = jnp.round(x * (TOP / peak)).astype(jnp.int32).astype(jnp.int16)
    return codes, peak * (1.0 / TOP)


def decode(codes, step):
    return codes.astype(jnp.int32).astype(jnp.float32) * step


class Group:
    def __init__(self, *copies):
        self.copies = copies

    def start(self):
        for copy in self.copies:
            copy.start()
        return self

    def wait_recv(self):
        for copy in self.copies:
            copy.wait_recv()

    def wait_send(self):
        for copy in self.copies:
            copy.wait_send()


def kernel(
    sizes, pos, count, blocks, right_in, left_in, old_in, right_out, gene_out, core_out,
    spots, code,
    tiles, dense, table, left, part, one_s, one_r, one_ss, one_sr, two_s, two_r, two_ss, two_sr,
    z_s, z_r, z_ss, z_sr, pieces, core_part, core_cell, cg_c, cg_d, cg_cs, cg_ds, cr_c, cr_d, cr_cs, cr_ds,
    core_code, core_step, gene_send, gene_recv,
    load_sem, agz_s, agz_r, agf_s, agx_s, agx_r, agd_s, agd_r, rsd_s, rsd_r, rs1_s, rs1_r, rs2_s, rs2_r, rsz_s, rsz_r,
    cc_s, cc_r, cgs_s, cgs_r, crs_s, crs_r, ar_s, ar_r, ag_s, ag_r, gs_s, gs_r,
):
    n_cell, n_gene, n_rank = sizes
    f32, bf16 = jnp.float32, jnp.bfloat16
    c, g, r = lax.axis_index("cell"), lax.axis_index("gene"), lax.axis_index("rank")
    b1, b0 = g // 2, g % 2
    gx = 2 * b1 + (1 - b0)
    gy = 2 * (1 - b1) + b0
    gd = 2 * (1 - b1) + (1 - b0)
    gene_peers = [gx, gy, gd]
    rows, width = part.shape
    quarter = rows // n_gene
    shard = quarter // n_rank
    half = width // 2
    lw = left_in.shape[0]
    left_width = left.shape[0]
    brows, bcols = tiles.shape[1], tiles.shape[2]
    gene_blocks = dense.shape[1] // bcols
    share = left_width // n_cell
    core_rows = share // n_gene
    lanes = width // n_rank

    def rank_of(k):
        return lax.rem(r + k, n_rank)

    def cell_of(k):
        return lax.rem(c + k, n_cell)

    def cut(start, step):
        return pl.ds(pl.multiple_of(start * step, step), step)

    def remote(src, dst, ssem, rsem, **where):
        device = (where.get("cell", c), where.get("gene", g), where.get("rank", r))
        return pltpu.make_async_remote_copy(
            src_ref=src, dst_ref=dst, send_sem=ssem, recv_sem=rsem,
            device_id=device, device_id_type=MESH,
        )

    def ship(codes, steps, ssem, rsem, **where):
        return Group(
            remote(*codes, ssem.at[0], rsem.at[0], **where),
            remote(*steps, ssem.at[1], rsem.at[1], **where),
        ).start()

    barrier = pltpu.get_barrier_semaphore()
    for k in range(1, n_rank):
        pl.semaphore_signal(barrier, inc=1, device_id=(c, g, rank_of(k)), device_id_type=MESH)
    for peer in gene_peers:
        pl.semaphore_signal(barrier, inc=1, device_id=(c, peer, r), device_id_type=MESH)
    for k in range(1, n_cell):
        pl.semaphore_signal(barrier, inc=1, device_id=(cell_of(k), g, r), device_id_type=MESH)

    load_tiles = pltpu.make_async_copy(blocks, tiles, load_sem.at[0])
    load_table = pltpu.make_async_copy(right_in, table, load_sem.at[1])
    load_tiles.start()
    load_table.start()
    own_left = pltpu.make_async_copy(left_in, left.at[cut(r, lw), :], load_sem.at[2])
    def note(s, spot):
        return jnp.where(lax.broadcasted_iota(jnp.int32, spot.shape, 1) == pos[0, 0, s], jnp.where(s < count[0, 0], s + 1, 0), spot)

    spots[...] = lax.fori_loop(0, tiles.shape[0], note, jnp.zeros(spots.shape, jnp.int32), unroll=8)
    load_code = pltpu.make_async_copy(spots, code, load_sem.at[4])
    load_code.start()
    load_old = pltpu.make_async_copy(old_in, gene_out, load_sem.at[3])

    pl.semaphore_wait(barrier, (n_rank - 1) + len(gene_peers) + (n_cell - 1))

    line = n_rank == 4
    direct = quarter // 2
    relay = (quarter - direct) // 2
    quarters = (cut(g, quarter), pl.ds(pl.multiple_of(gd * quarter, quarter), direct))

    def rank_pieces(i, act):
        for near in (False, True) if line else (True,):
            for z in range(n_rank):
                rank_piece(i, z, act, near)

    def rank_piece(i, z, act, near):
        if line:
            wanted = (z - r == 1) | (r - z == 1) if near else (z - r == 2) | (r - z == 2)
        else:
            wanted = z != r

        @pl.when(wanted)
        def _():
            at = quarters[i]
            act(remote(left_in.at[:, at], left.at[cut(r, lw), at], agz_s.at[i, z], agz_r.at[i, r], rank=z))

    def rank_arrival(i, z):
        here = left.at[cut(z, lw), quarters[i]]
        return remote(here, here, agz_s.at[i, z], agz_r.at[i, z], rank=z)

    def rank_wait(i, z):
        passed = ((r == 2) & (z == 0)) | ((r == 1) & (z == 3)) if line else r < 0

        @pl.when((z != r) & jnp.logical_not(passed))
        def _():
            rank_arrival(i, z).wait_recv()

    def rank_pass(i, act):
        for via, source, target in ((2, 0, 3), (1, 3, 0)) if line else ():

            @pl.when(r == via)
            def _():
                here = left.at[cut(source, lw), quarters[i]]
                act(source, remote(here, here, agf_s.at[i], agz_r.at[i, source], rank=target))

    def pass_on(i):
        def go(source, copy):
            rank_arrival(i, source).wait_recv()
            copy.start()

        rank_pass(i, go)

    def start(copy):
        copy.start()

    def wait_recv(copy):
        copy.wait_recv()

    def wait_send(copy):
        copy.wait_send()

    rank_pieces(0, start)
    load_tiles.wait()
    load_table.wait()
    load_code.wait()
    own_left.start()
    load_old.start()

    row_blocks = quarter // brows
    group = min(8, gene_blocks)

    def compute(q, first=0, last=2):
        def fill(i, carry):
            for u in range(group):
                at = i * group + u
                rb = q * row_blocks + at // gene_blocks
                gb = at % gene_blocks
                slot = code[0, rb * gene_blocks + gb]
                block = tiles[jnp.maximum(slot - 1, 0)]
                dense[cut(rb, brows), cut(gb, bcols)] = jnp.where(slot > 0, block, jnp.zeros_like(block))
            return carry

        steps = row_blocks * gene_blocks // group // 2
        lax.fori_loop(first * steps, last * steps, fill, 0)

        def multiply(h, carry):
            here = pl.ds(pl.multiple_of(q * quarter + h * (quarter // 2), quarter // 2), quarter // 2)
            part[here, :] = jnp.dot(dense[here, :], table[...], preferred_element_type=f32)
            return carry

        lax.fori_loop(first, last, multiply, 0)

    h0, h1 = pl.ds(0, half), pl.ds(half, half)

    def shard_of(q, z):
        return pl.ds(pl.multiple_of(q * quarter + z * shard, shard), shard)

    order = [rank_of(k) for k in range(1, n_rank)] + [r]

    def rs1_shards(i, q, h, peer, some):
        copies = []
        for z in some:
            j = z
            at = cut(z, shard)
            one_s[i, at, :], one_ss[i, z] = encode(part[shard_of(q, z), h])
            copies.append(
                ship(
                    (one_s.at[i, at, :], one_r.at[i, at, :]), (one_ss.at[i, z], one_sr.at[i, z]),
                    rsd_s.at[i * n_rank + j], rsd_r.at[i * n_rank + j], gene=peer,
                )
            )
        return copies

    def rs1(i, q, h, peer):
        def pack(z, carry):
            one_s[i, cut(z, shard), :], one_ss[i, z] = encode(part[shard_of(q, z), h])
            return carry

        lax.fori_loop(0, n_rank, pack, 0)
        return ship(
            (one_s.at[i], one_r.at[i]), (one_ss.at[i], one_sr.at[i]), rs1_s.at[i - 2], rs1_r.at[i - 2], gene=peer
        )

    def first_hop(i, z):
        return decode(one_r[i, cut(z, shard), :], one_sr[i, z])

    def second_hop(i, z):
        return decode(two_r[i, cut(z, shard), :], two_sr[i, z])

    d0, d1 = [], []
    middle = n_rank // 2
    for at, some in enumerate((range(middle), range(middle, n_rank))):
        compute(gd, at, at + 1)
        d0 += rs1_shards(0, gd, h0, gx, some)
        d1 += rs1_shards(1, gd, h1, gy, some)
    compute(gx)
    o0 = rs1(2, gx, h0, gx)
    compute(gy)
    o1 = rs1(3, gy, h1, gy)
    own_left.wait()
    pass_on(0)
    rank_pieces(1, start)

    second = [[], []]
    for z in range(n_rank):
        for i, (first, q, h, peer) in enumerate(((d0, gy, h0, gy), (d1, gx, h1, gx))):
            first[z].wait_recv()
            at = cut(z, shard)
            two_s[i, at, :], two_ss[i, z] = encode(part[shard_of(q, z), h] + first_hop(i, z))
            second[i].append(
                ship(
                    (two_s.at[i, at, :], two_r.at[i, at, :]), (two_ss.at[i, z], two_sr.at[i, z]),
                    rs2_s.at[i * n_rank + z], rs2_r.at[i * n_rank + z], gene=peer,
                )
            )

    compute(g)
    per_share = 0 if n_rank % n_cell else n_rank // n_cell
    lead = n_rank - per_share
    base = (c + 1) * per_share

    def slice_of(j):
        return lax.rem(base + j, n_rank)

    def left_piece(j, act):
        z = slice_of(j)
        here = left.at[cut(z, lw), cut(g, quarter)]

        @pl.when(z != r)
        def _():
            for i, peer in enumerate((gx, gy)):
                act(remote(here, here, agx_s.at[j, i], agx_r.at[j, i], gene=peer))

    def left_corner(j, act):
        z = slice_of(j)

        @pl.when(z != r)
        def _():
            for i, (q, peer) in enumerate(((gy, gx), (gx, gy))):
                here = left.at[cut(z, lw), pl.ds(pl.multiple_of(q * quarter + direct + i * relay, relay), relay)]
                act(remote(here, here, agd_s.at[j, i], agd_r.at[j, i], gene=peer))

    for j in range(lead):
        rank_wait(0, slice_of(j))
        left_piece(j, start)

    o0.wait_recv()
    o1.wait_recv()
    rsz = []
    for copy in second[0] + second[1]:
        copy.wait_recv()
    for j, z in enumerate(order):
        here = shard_of(g, z)
        part[here, h0] = part[here, h0] + first_hop(2, z) + second_hop(0, z)
        part[here, h1] = part[here, h1] + first_hop(3, z) + second_hop(1, z)
        if j < n_rank - 1:
            z_s[j], z_ss[j] = encode(part[here, :])
            rsz.append(
                ship((z_s.at[j], z_r.at[j]), (z_ss.at[j], z_sr.at[j]), rsz_s.at[j], rsz_r.at[j], rank=z)
            )
        mine = part[here, :]
        high = mine.astype(bf16)
        pieces[0, cut(z, shard), :] = high
        pieces[1, cut(z, shard), :] = (mine - high.astype(f32)).astype(bf16)

    for j in range(lead, n_rank):
        rank_wait(0, slice_of(j))

    def core_rows_of(k):
        at = cut(cell_of(k), share)

        def multiply(h, carry):
            here = cut(h, half)
            rows_left = left[at, cut(g, quarter)]
            core_part[at, here] = jnp.dot(rows_left, pieces[0, :, here], preferred_element_type=f32) + jnp.dot(
                rows_left, pieces[1, :, here], preferred_element_type=f32
            )
            return carry

        lax.fori_loop(0, 2, multiply, 0)

    own_share = cut(c, share)
    cc = []
    for k in range(1, n_cell):
        core_rows_of(k)
        copy = remote(
            core_part.at[cut(cell_of(k), share), :], core_cell.at[k - 1],
            cc_s.at[k - 1], cc_r.at[k - 1], cell=cell_of(k),
        )
        copy.start()
        cc.append(copy)
    core_rows_of(0)
    for k in range(1, n_cell):
        cc[k - 1].wait_recv()
        core_part[own_share, :] = core_part[own_share, :] + core_cell[k - 1]
    coded = core_code.dtype == jnp.int16

    def pack(x):
        return encode(x) if coded else (x, jnp.ones((1, x.shape[1]), f32))

    def unpack(x, step):
        return decode(x, step) if coded else x

    cg = []
    for i, peer in reversed(list(enumerate(gene_peers))):
        src = pl.ds(pl.multiple_of(c * share + peer * core_rows, 8), core_rows)
        cg_c[i], cg_cs[i] = pack(core_part[src, :])
        cg.append(ship((cg_c.at[i], cg_d.at[i]), (cg_cs.at[i], cg_ds.at[i]), cgs_s.at[i], cgs_r.at[i], gene=peer))
    for j in range(lead, n_rank):
        left_piece(j, start)
    pass_on(1)

    own_rows = pl.ds(pl.multiple_of(c * share + g * core_rows, 8), core_rows)
    for i in range(len(gene_peers)):
        cg[-1 - i].wait_recv()
        core_part[own_rows, :] = core_part[own_rows, :] + unpack(cg_d[i], cg_ds[i])
    cr = []
    for k in range(1, n_rank):
        cr_c[k - 1], cr_cs[k - 1] = pack(core_part[own_rows, cut(rank_of(k), lanes)])
        cr.append(
            ship(
                (cr_c.at[k - 1], cr_d.at[k - 1]), (cr_cs.at[k - 1], cr_ds.at[k - 1]),
                crs_s.at[k - 1], crs_r.at[k - 1], rank=rank_of(k),
            )
        )

    for j in range(lead):
        left_piece(j, wait_recv)
        left_corner(j, start)

    final = core_part[own_rows, cut(r, lanes)]
    for k in range(1, n_rank):
        cr[k - 1].wait_recv()
        final = final + unpack(cr_d[k - 1], cr_ds[k - 1])
    out_rows = pl.ds(pl.multiple_of(g * core_rows, 8), core_rows)
    core_code[out_rows, cut(r, lanes)], core_step[g, :, cut(r, lanes)] = pack(final)

    def core_piece(z, ssem, rsem, **where):
        piece = core_code.at[out_rows, cut(z, lanes)]
        step = core_step.at[g, :, cut(z, lanes)]
        return ship((piece, piece), (step, step), ssem, rsem, **where)

    ar = [core_piece(r, ar_s.at[k - 1], ar_r.at[k - 1], rank=rank_of(k)) for k in range(1, n_rank)]
    ag = []

    def spread(k):
        for i, peer in reversed(list(enumerate(gene_peers))):
            ag.append(core_piece(rank_of(n_rank - k), ag_s.at[k, i], ag_r.at[k, i], gene=peer))

    spread(0)
    for j in range(lead, n_rank):
        left_piece(j, wait_recv)
        left_corner(j, start)
    for j in range(lead):
        rank_wait(1, slice_of(j))
        left_corner(j, wait_recv)

    chunks = dense.shape[1] // GENE_CHUNK

    def gene_copy(k, j):
        return remote(
            gene_send.at[k - 1, :, cut(j, GENE_CHUNK)], gene_recv.at[k - 1, :, cut(j, GENE_CHUNK)],
            gs_s.at[k - 1, j], gs_r.at[k - 1, j], cell=cell_of(k),
        )

    for k in range(1, n_cell):
        peer_rows = cut(cell_of(k), share)

        def send_chunk(j, carry):
            gene_send[k - 1, :, cut(j, GENE_CHUNK)] = jnp.dot(
                left[peer_rows, :], dense[:, cut(j, GENE_CHUNK)], preferred_element_type=f32
            )
            gene_copy(k, j).start()
            return carry

        lax.fori_loop(0, chunks, send_chunk, 0)

    for k in range(1, n_rank):
        ar[k - 1].wait_recv()
        spread(k)
    for copy in rsz:
        copy.wait_recv()
    mine = part[shard_of(g, r), :]
    for j in range(n_rank - 1):
        mine = mine + decode(z_r[j], z_sr[j])
    right_out[...] = mine
    load_old.wait()

    def own_dot(q, here):
        return jnp.dot(
            left[own_share, cut(q, quarter)], dense[cut(q, quarter), here], preferred_element_type=f32
        )

    def own_chunk(j, carry):
        here = cut(j, GENE_CHUNK)
        gene_out[:, here] = gene_out[:, here] + own_dot(g, here) + own_dot(gx, here) + own_dot(gy, here)
        return carry

    lax.fori_loop(0, chunks, own_chunk, 0)

    for j in range(lead, n_rank):
        rank_wait(1, slice_of(j))
    for j in range(lead, n_rank):
        left_corner(j, wait_recv)

    def last_chunk(j, carry):
        here = cut(j, GENE_CHUNK)
        for k in range(1, n_cell):
            gene_copy(k, j).wait_recv()
        total = gene_out[:, here] + own_dot(gd, here)
        for k in range(1, n_cell):
            total = total + gene_recv[k - 1, :, here]
        gene_out[:, here] = total
        return carry

    lax.fori_loop(0, chunks, last_chunk, 0)

    for copy in ag:
        copy.wait_recv()
    for i in range(n_gene):
        at = pl.ds(i * core_rows, core_rows)
        core_out[at, :] = unpack(core_code[at, :], core_step[i])


    for copy in d0 + d1 + [o0, o1] + second[0] + second[1] + rsz + cc + cg + cr + ar + ag:
        copy.wait_send()
    for j in range(n_rank):
        left_piece(j, wait_send)
        left_corner(j, wait_send)
    for i in range(2):
        rank_pieces(i, wait_send)
        rank_pass(i, lambda source, copy: copy.wait_send())
    for k in range(1, n_cell):

        def drain(j, carry):
            gene_copy(k, j).wait_send()
            return carry

        lax.fori_loop(0, chunks, drain, 0)


def body(sizes, blocks, block_pos, block_count, test_right, test_left, gene_sketch_old):
    n_cell, n_gene, n_rank = sizes
    f32, bf16, i16 = jnp.float32, jnp.bfloat16, jnp.int16
    tiles = blocks[0, 0]
    slots, brows, bcols = tiles.shape
    genes, width = test_right.shape
    rows, lw = test_left.shape
    left_width = lw * n_rank
    gene_blocks = genes // bcols
    places = (rows // brows) * gene_blocks
    quarter, half = rows // n_gene, width // 2
    shard = quarter // n_rank
    share = left_width // n_cell
    core_rows, lanes = share // n_gene, width // n_rank
    chunks = genes // GENE_CHUNK
    dma = pltpu.SemaphoreType.DMA
    vmem = pltpu.VMEM
    z, x = n_rank - 1, n_gene - 1
    wire = f32 if core_rows % 16 else i16

    def pair(*shape):
        return [dma(shape), dma(shape)]

    def both(shape, kind):
        return [vmem(shape, kind), vmem(shape, kind)]

    outs = (
        jax.ShapeDtypeStruct((shard, width), f32),
        jax.ShapeDtypeStruct((share, genes), f32),
        jax.ShapeDtypeStruct((share, width), f32),
    )
    return pl.pallas_call(
        functools.partial(kernel, sizes),
        out_shape=tuple(pltpu.VMEM(o.shape, o.dtype) for o in outs),
        in_specs=[pl.BlockSpec(memory_space=pltpu.SMEM)] * 2 + [pl.BlockSpec(memory_space=pltpu.HBM)] * 4,
        out_specs=tuple(pl.BlockSpec(memory_space=pltpu.VMEM) for _ in range(3)),
        scratch_shapes=[
            vmem((1, places), jnp.int32),
            pltpu.SMEM((1, places), jnp.int32),
            vmem((slots, brows, bcols), bf16),
            vmem((rows, genes), bf16),
            vmem((genes, width), bf16),
            vmem((left_width, rows), bf16),
            vmem((rows, width), f32),
            *both((4, quarter, half), i16),
            *both((4, n_rank, 1, half), f32),
            *both((2, quarter, half), i16),
            *both((2, n_rank, 1, half), f32),
            *both((z, shard, width), i16),
            *both((z, 1, width), f32),
            vmem((2, quarter, width), bf16),
            vmem((left_width, width), f32),
            vmem((n_cell - 1, share, width), f32),
            *both((x, core_rows, width), wire),
            *both((x, 1, width), f32),
            *both((z, core_rows, lanes), wire),
            *both((z, 1, lanes), f32),
            vmem((share, width), wire),
            vmem((n_gene, 1, width), f32),
            vmem((n_cell - 1, share, genes), f32),
            vmem((n_cell - 1, share, genes), f32),
            dma((5,)),
            *pair(2, n_rank),
            dma((2,)),
            *pair(n_rank, 2),
            *pair(n_rank, 2),
            *pair(2 * n_rank, 2),
            *pair(2, 2),
            *pair(2 * n_rank, 2),
            *pair(z, 2),
            *pair(n_cell - 1),
            *pair(x, 2),
            *pair(z, 2),
            *pair(z, 2),
            *pair(n_rank, x, 2),
            *pair(n_cell - 1, chunks),
        ],
        compiler_params=pltpu.CompilerParams(
            collective_id=0, has_side_effects=True, vmem_limit_bytes=56 * 1024 * 1024
        ),
        name="sketch",
    )(block_pos, block_count, tiles, test_right, test_left.T, gene_sketch_old)


def solution(mesh):
    sizes = tuple(mesh.shape[name] for name in ("cell", "gene", "rank"))
    return jax.shard_map(
        functools.partial(body, sizes),
        mesh=mesh,
        in_specs=(
            P("cell", ("gene", "rank"), None, None, None),
            P("cell", ("gene", "rank"), None),
            P("cell", ("gene", "rank")),
            P(("gene", "rank"), None),
            P("cell", "rank"),
            P("cell", ("gene", "rank")),
        ),
        out_specs=(P(("cell", "gene", "rank"), None), P("cell", ("gene", "rank")), P("cell", None)),
        check_vma=False,
    )
```
